256 devices in a mesh: dp: 8 (over x, core), ctx: 32 (over z, y).
Axes of the slice: x: 4, y: 4, z: 8, core: 2. Of those that a mesh axis runs over, the one named last changes fastest.
Arguments:
- tokens: bfloat16 [8, 4096, 4096], P('dp', 'ctx'), may hold values from -6 to 6
- qk_weight: bfloat16 [4096, 512], replicated, may hold values from -0.09375 to 0.09375
- conv_weight: float32 [3, 512], replicated, may hold values from -3 to 3
- values: bfloat16 [8, 4096, 2048], P('dp', 'ctx'), may hold values from -6 to 6
- cotangent: bfloat16 [8, 4096, 2048], P('dp', 'ctx'), may hold values from -6 to 6
Outputs:
- mixed_out: bfloat16 [8, 4096, 2048], P('dp', 'ctx')
- grad_tokens: bfloat16 [8, 4096, 4096], P('dp', 'ctx')
- grad_values: bfloat16 [8, 4096, 2048], P('dp', 'ctx')
- grad_qk_weight: float32 [4096, 512], P('ctx')
The draws below stay inside these ranges and needn't reach their ends.
All inputs are finite; a program needn't handle non-finite values.
Results may differ from the reference program's by a relative error of at most 0.04.
Values sent between devices are 32-bit elements; how exact they have to be, the bound alone decides.
No kernel may reach another device: no remote copies, remote signals or barrier semaphores. Data moves between devices by JAX's collectives and lax.ppermute only.
A program may use at most 128 MiB of HBM per device.

```python
import jax
import jax.numpy as jnp
import numpy as np
from jax import lax

D = 4096
H = 16
F = 16
V = 128
KW = 3
TOK_DEV = 128
E = 153
TOKENS = 4096
SEQS = 8


def draw_values(key, part):
    noise_key, offset_key = jax.random.split(jax.random.fold_in(key, 7))
    blocks = TOKENS // TOK_DEV
    offset = jax.random.normal(offset_key, (SEQS, blocks, 1, H * V), jnp.float32)
    noise = 0.8 * jax.random.normal(noise_key, (SEQS, blocks, TOK_DEV, H * V), jnp.float32)
    result = jnp.clip(noise + 0.8 * offset, -6.0, 6.0)
    return result.reshape(SEQS, TOKENS, H * V).astype(jnp.bfloat16)


def strengthened(values, stream_key, source, target, parts, factor):
    def block_of(axis_at):
        return (jnp.arange(values.shape[axis_at]) // (values.shape[axis_at] // parts)).reshape((-1,) + (1,) * (values.ndim - 1 - axis_at))

    first = jax.random.permutation(stream_key, parts)[block_of(target)]
    second = (block_of(target) + parts // 2) % parts
    return jnp.where((block_of(source) == first) | (block_of(source) == second), factor * values, values)


def steps_of(rng, dims, shards, low, high):
    factor_of = 1.0
    for dim, shards_of in shards:
        draws = jax.random.uniform(jax.random.fold_in(jax.random.fold_in(rng, 6), dim), (shards_of,), jnp.float32, low / len(shards), high / len(shards))
        factor_of = factor_of * jnp.repeat(jnp.exp(draws), dims[dim] // shards_of).reshape((-1,) + (1,) * (len(dims) - 1 - dim))
    return factor_of


def bell_draw(rng, shape, scale, most, cuts=(), held_as=jnp.bfloat16):
    values = scale * jax.random.normal(rng, shape, jnp.float32)
    if cuts:
        values = values * steps_of(rng, shape, cuts, -0.22, 0.18)
    return jnp.clip(values, -most, most).astype(held_as)


def heavy_noise(key, extent, deviation, most, cuts, heavy, kind=jnp.bfloat16):
    drawn = deviation * jax.random.normal(key, extent, jnp.float32)
    if cuts:
        drawn = drawn * steps_of(key, extent, cuts, -0.22, 0.18)
    return jnp.clip(strengthened(drawn, jax.random.fold_in(key, 3), *heavy), -most, most).astype(kind)


def setup_inputs(seed: int = 0) -> dict:
    keys = jax.random.split(jax.random.key(seed), 6)
    return {
        "tokens": heavy_noise(keys[0], (SEQS, TOKENS, D), 1.0, 6.0, ((0, 8), (1, 32)), (1, 2, 32, 2.75)),
        "qk_weight": bell_draw(keys[1], (D, 2 * H * F), D ** -0.5, 0.09375),
        "conv_weight": bell_draw(keys[2], (KW, 2 * H * F), 0.6, 3.0, (), jnp.float32),
        "values": draw_values(jax.random.fold_in(keys[5], 71), 0),
        "cotangent": bell_draw(keys[4], (SEQS, TOKENS, H * V), 1.0, 6.0, ((0, 8), (1, 32))),
    }


def product(form, left, right):
    return jnp.einsum(form, left.astype(jnp.float32), right.astype(jnp.float32), precision=lax.Precision.HIGHEST)

def taylor_map(inputs):
    size = inputs.shape[1]
    pieces = [jnp.ones_like(inputs[:, :1]), inputs * size ** (-0.25)]
    for first in range(size):
        scale = np.full((size - first, 1), 1.0 / np.sqrt(size), np.float32)
        scale[0, 0] = 1.0 / np.sqrt(2.0 * size)
        pieces.append(inputs[:, first:first + 1] * inputs[:, first:] * scale)
    return jnp.concatenate(pieces, 1).astype(jnp.bfloat16)

def features_of(extended, conv_weight):
    taps = conv_weight.shape[0]
    length = extended.shape[0] - taps + 1
    mixed = conv_weight[0] * extended[taps - 1:]
    for offset in range(1, taps):
        mixed = mixed + conv_weight[offset] * extended[taps - 1 - offset:taps - 1 - offset + length]
    half = mixed.shape[1] // 2
    query = jnp.transpose(mixed[:, :half].reshape(length, H, F), (1, 2, 0))
    key_part = jnp.transpose(mixed[:, half:].reshape(length, H, F), (1, 2, 0))
    return (taylor_map(query), taylor_map(key_part))

def block_state(key_feat, values32):
    values_bf = values32.astype(jnp.bfloat16)
    state = product('het,thv->hev', key_feat, values_bf)
    return (state, lax.optimization_barrier(jnp.sum(key_feat.astype(jnp.float32), -1)))

def block_output(query_feat, key_feat, values32, carried, carried_total):
    length = query_feat.shape[-1]
    values_bf = values32.astype(jnp.bfloat16)
    causal = jnp.tril(jnp.ones((length, length), jnp.float32))
    scores = product('het,hes->hts', query_feat, key_feat) * causal
    local_sum = lax.optimization_barrier(jnp.sum(scores, -1))
    numer = product('hts,shv->thv', scores.astype(jnp.bfloat16), values_bf)
    numer = numer + product('het,hev->thv', query_feat, carried.astype(jnp.bfloat16))
    denom = jnp.transpose(local_sum) + jnp.einsum('het,he->th', query_feat.astype(jnp.float32), carried_total, precision=lax.Precision.HIGHEST)
    return (numer / denom[..., None]).reshape(length, -1)

def mixer(projected, conv_weight, values32):
    padding = jnp.zeros((KW - 1, projected.shape[1]), projected.dtype)
    query_feat, key_feat = features_of(jnp.concatenate([padding, projected], 0), conv_weight)
    blocks = TOKENS // TOK_DEV
    query_blocks = jnp.transpose(query_feat.reshape(H, E, blocks, TOK_DEV), (2, 0, 1, 3))
    key_blocks = jnp.transpose(key_feat.reshape(H, E, blocks, TOK_DEV), (2, 0, 1, 3))
    value_blocks = values32.reshape(blocks, TOK_DEV, H, V)
    states, totals = jax.vmap(block_state)(key_blocks, value_blocks)
    carried = jnp.concatenate([jnp.zeros_like(states[:1]), jnp.cumsum(states, 0)[:-1]], 0)
    carried_total = jnp.concatenate([jnp.zeros_like(totals[:1]), jnp.cumsum(totals, 0)[:-1]], 0)
    result = jax.vmap(block_output)(query_blocks, key_blocks, value_blocks, carried, carried_total)
    return result.reshape(TOKENS, H * V)

def reference(tokens, qk_weight, conv_weight, values, cotangent):

    def one_sequence(inputs):
        local_x, local_values, local_grad = inputs
        projected = jnp.dot(local_x, qk_weight, preferred_element_type=jnp.float32)
        values32 = local_values.astype(jnp.float32)
        result, pullback = jax.vjp(lambda proj_in, val_in: mixer(proj_in, conv_weight, val_in), projected, values32)
        grad_proj, grad_vals = pullback(local_grad.astype(jnp.float32))
        grad_bf = grad_proj.astype(jnp.bfloat16)
        grad_x = lax.dot_general(grad_bf, qk_weight, (((1,), (1,)), ((), ())), preferred_element_type=jnp.float32).astype(jnp.bfloat16)
        weight_term = lax.dot_general(local_x, grad_bf, (((0,), (0,)), ((), ())), preferred_element_type=jnp.float32)
        return (result.astype(jnp.bfloat16), grad_x, grad_vals.astype(jnp.bfloat16), weight_term)
    results = lax.map(one_sequence, (tokens, values, cotangent))
    return (results[0], results[1], results[2], lax.optimization_barrier(jnp.sum(results[3], 0)))
```

```python
import jax
import jax.numpy as jnp
import numpy as np
from jax import lax
from jax.experimental import pallas as pl
from jax.experimental.pallas import tpu as pltpu
from jax.sharding import Mesh, PartitionSpec as P

H = 16
F = 16
V = 128
NX, NC, NZ, NY = 4, 2, 8, 4
T = 128
TS = T * NY
HG = H // NY
E = 160
EP = 256
f32 = jnp.float32
bf16 = jnp.bfloat16


def feature_tables():
    first = np.zeros((128, 512), np.float32)
    weight = np.zeros((8, EP), np.float32)
    for f in range(128):
        i, d = f % 16, f // 16
        first[i, f] = 1
        first[(i + d) % 16, 128 + f] = 1
        weight[:, f] = 1 / 32 if d == 0 else 1 / 16
    for f in range(8):
        first[f, 256 + f] = 1
        first[f + 8, 384 + f] = 1
        weight[:, 128 + f] = 1 / 16
    for f in range(16):
        first[f, 256 + 8 + f] = 1
        first[16, 384 + 8 + f] = 0.5
        weight[:, 128 + 8 + f] = 1 / 4
    first[16, 256 + 24] = 0.5
    first[16, 384 + 24] = 0.5
    weight[:, 128 + 24] = 1
    sel_q = first.copy()
    sel_q[64:80] = first[:16]
    sel_k = first.copy()
    sel_k[32:48] = first[:16]
    return sel_q, sel_k, weight


SEL_Q, SEL_K, WEIGHT = feature_tables()


def mm(a, b):
    return lax.dot_general(a, b, (((1,), (0,)), ((), ())), preferred_element_type=f32)


def mm_nt(a, b):
    return lax.dot_general(a, b, (((1,), (1,)), ((), ())), preferred_element_type=f32)


def mm_tn(a, b):
    return lax.dot_general(a, b, (((0,), (0,)), ((), ())), preferred_element_type=f32)


def run(kernel, outs, *args, scratch=()):
    vm = pl.BlockSpec(memory_space=pltpu.VMEM)
    return pl.pallas_call(
        kernel,
        out_shape=[jax.ShapeDtypeStruct(s, d) for s, d in outs],
        in_specs=[vm] * len(args),
        out_specs=[vm] * len(outs),
        scratch_shapes=list(scratch),
        compiler_params=pltpu.CompilerParams(vmem_limit_bytes=24 << 20),
    )(*args)


def features(u, sel):
    x = mm(u, sel)
    return jnp.concatenate([x[:, :128] * x[:, 128:256], x[:, 256:384] * x[:, 384:]], 1)


def feature_grad(u, sel, grad):
    x = mm(u, sel)
    g1, g2 = grad[:, :128], grad[:, 128:]
    stacked = jnp.concatenate(
        [g1 * x[:, 128:256], g1 * x[:, :128], g2 * x[:, 384:], g2 * x[:, 256:384]], 1
    ).astype(bf16)
    return mm_nt(stacked, sel)


def causal(rows, r):
    row = lax.broadcasted_iota(jnp.int32, (T, rows), 0) + r * T
    col = lax.broadcasted_iota(jnp.int32, (T, rows), 1)
    return row >= col


def prepare_kernel(mg, sel_k, w, uq, uk, tot, rs):
    lane = lax.broadcasted_iota(jnp.int32, (TS, 128), 1)
    tot[...] = jnp.zeros_like(tot)
    m = mg[...]
    for h in range(HG):
        for is_key in (0, 1):
            x = pltpu.roll(m, (128 - 64 * is_key - 16 * h) % 128, 1)
            hi = x.astype(bf16).astype(f32)
            lo = x - hi
            a, b = (lo, hi) if is_key else (hi, lo)
            u = jnp.where(lane < 16, hi, jnp.where(lane == 16, 2.0, 0.0))
            u = jnp.where((lane >= 32) & (lane < 48), pltpu.roll(a, 32, 1), u)
            u = jnp.where((lane >= 64) & (lane < 80), pltpu.roll(b, 64, 1), u)
            (uk if is_key else uq)[h] = u.astype(bf16)
        rk = features(uk[h], sel_k[...])
        tot[h : h + 1] = jnp.sum(rk, 0, keepdims=True) * w[0:1]
        for r in range(NY):
            rows = (r + 1) * T
            s = mm_nt(uq[h, r * T : rows], uk[h, :rows])
            p = jnp.where(causal(rows, r), 0.5 + s * s * (1 / 32), 0.0)
            rs[r * T : rows, h : h + 1] = jnp.sum(p, 1, keepdims=True)


def state_kernel(uk, v, sel_k, w, state, vb):
    vb[...] = v[...].astype(bf16)
    for h in range(HG):
        rk = (features(uk[h], sel_k[...]) * w[0:1]).astype(bf16)
        s = mm_tn(rk, vb[:, h * V : (h + 1) * V])
        state[h * E : (h + 1) * E] = s[:E]


def denom_kernel(uq, rs, etot, cot, sel_q, w, dn, inv, gs):
    for h in range(HG):
        cols = slice(h * V, (h + 1) * V)
        rq = features(uq[h], sel_q[...])
        den = rs[:, h : h + 1] + jnp.sum(rq * etot[h : h + 1], 1, keepdims=True)
        iv = 1.0 / den
        inv[:, h : h + 1] = iv
        d = (cot[:, cols] * iv).astype(bf16)
        dn[:, cols] = d
        s = mm_tn((rq * w[0:1]).astype(bf16), d)
        gs[h * E : (h + 1) * E] = s[:E]


def padded_state(ref, h):
    return jnp.concatenate(
        [ref[h * E : (h + 1) * E], jnp.zeros((EP - E, V), f32)], 0
    ).astype(bf16)


def local_kernel(
    uq, uk, vb, dn, inv, etot, carried, sel_q, w, out, dq, gv, dk, gtot, dk_acc
):
    lane = lax.broadcasted_iota(jnp.int32, (T, 128), 1)
    lane_all = lax.broadcasted_iota(jnp.int32, (TS, 128), 1)
    gtot[...] = jnp.zeros_like(gtot)
    dq[...] = jnp.zeros_like(dq)
    dk[...] = jnp.zeros_like(dk)
    for h in range(HG):
        cols = slice(h * V, (h + 1) * V)
        c = padded_state(carried, h)
        for r in reversed(range(NY)):
            rows = (r + 1) * T
            mine = slice(r * T, rows)
            u = uq[h, mine]
            keep = causal(rows, r)
            s = mm_nt(u, uk[h, :rows])
            p = jnp.where(keep, 0.5 + s * s * (1 / 32), 0.0).astype(bf16)
            rq = features(u, sel_q[...])
            numer = mm(p, vb[:rows, cols]) + mm(rq.astype(bf16), c)
            o = numer * inv[mine, h : h + 1]
            out[mine, cols] = o
            d = dn[mine, cols]
            dd = -jnp.sum(d.astype(f32) * o, 1, keepdims=True)
            dp = mm_nt(d, vb[:rows, cols]) + dd
            ds = jnp.where(keep, dp * s * (1 / 16), 0.0).astype(bf16)
            gtot[h : h + 1] += jnp.sum(rq * dd, 0, keepdims=True) * w[0:1]
            dr = mm_nt(d, c) + dd * etot[h : h + 1]
            g = mm(ds, uk[h, :rows]) + feature_grad(u, sel_q[...], dr)
            dq[mine] += pltpu.roll(jnp.where(lane < 16, g, 0.0), 16 * h, 1)
            gv_add = mm_tn(p, d)
            dk_add = mm_tn(ds, u)
            if r == NY - 1:
                gv[:, cols] = gv_add
                dk_acc[...] = dk_add
            else:
                gv[:rows, cols] += gv_add
                dk_acc[:rows] += dk_add
        dk[...] += pltpu.roll(
            jnp.where(lane_all < 16, dk_acc[...], 0.0), 64 + 16 * h, 1
        )


def key_kernel(uk, vb, gv_in, dq, dk, gcar, egtot, sel_k, gv, gm):
    lane = lax.broadcasted_iota(jnp.int32, (TS, 128), 1)
    total = dq[...] + dk[...]
    for h in range(HG):
        cols = slice(h * V, (h + 1) * V)
        c = padded_state(gcar, h)
        rk = features(uk[h], sel_k[...]).astype(bf16)
        gv[:, cols] = gv_in[:, cols] + mm(rk, c)
        dr = mm_nt(vb[:, cols], c) + egtot[h : h + 1]
        g = feature_grad(uk[h], sel_k[...], dr)
        total += pltpu.roll(jnp.where(lane < 16, g, 0.0), 64 + 16 * h, 1)
    gm[...] = total


def conv_kernel(y, g0, g1, g2, g3, h0, h1, h2, h3, cw, gp, pad):
    for s, (g, halo) in enumerate(((g0, h0), (g1, h1), (g2, h2), (g3, h3))):
        group = lax.rem(y[0] - s + NY, NY)
        pad[:TS] = g[...]
        pad[TS:] = halo[...]
        at = pl.ds(pl.multiple_of(group * 128, 128), 128)
        total = g[...] * cw[0:1, at]
        for j in (1, 2):
            total += pad[j : TS + j] * cw[j : j + 1, at]
        gp[:, at] = total.astype(bf16)


def rows_kernel(back, rows):
    for j in range(NY):
        rows[:, j * HG * V : (j + 1) * HG * V] = back[j].astype(bf16)


def transpose_kernel(a, flipped):
    for j in range(NY):
        flipped[:, j * T : (j + 1) * T] = jnp.transpose(a[j * T : (j + 1) * T]).astype(bf16)


def shift(value, axis, by):
    n = lax.axis_size(axis)
    return lax.ppermute(value, axis, [(i, (i + by) % n) for i in range(n)])


def shift_open(value, axis, by):
    n = lax.axis_size(axis)
    return lax.ppermute(
        value, axis, [(i, i + by) for i in range(n) if 0 <= i + by < n]
    )


def totals_scan(tot, sign):
    near = sum(shift_open(tot, "z", sign * s) for s in (1, 2, 3))
    far = shift_open(near + tot, "z", sign * 4)
    return near + far


def state_scan(state, sign):
    z = lax.axis_index("z")
    gathered = lax.all_gather(state, "z")
    order = lax.broadcasted_iota(jnp.int32, (NZ, 1, 1), 0)
    keep = order < z if sign > 0 else order > z
    return jnp.sum(jnp.where(keep, gathered, 0.0), 0)


def swap_y(value):
    return lax.all_to_all(value, "y", 0, 0, tiled=True)


def by_group(value):
    rows = value.shape[0]
    return jnp.transpose(value.reshape(rows, 2, NY, 64), (2, 0, 1, 3)).reshape(NY, rows, 128)


def on_device(tokens, qk_weight, conv_weight, values, cotangent):
    y = lax.axis_index("y")
    x = lax.axis_index("x")
    core = lax.axis_index("core")
    z = lax.axis_index("z")
    sel_q, sel_k = jnp.asarray(SEL_Q, bf16), jnp.asarray(SEL_K, bf16)
    w = jnp.asarray(WEIGHT, f32)
    local_x = tokens[0]

    def head_groups(a):
        return jnp.transpose(a.reshape(T, NY, HG * V), (1, 0, 2)).astype(f32)

    v_all = swap_y(head_groups(values[0])).reshape(TS, HG * V)
    projected = jnp.dot(local_x, qk_weight, preferred_element_type=f32)
    halo = lax.ppermute(
        projected[T - 2 :], ("z", "y"), [(i, i + 1) for i in range(NZ * NY - 1)]
    )
    ext = jnp.concatenate([halo, projected], 0)
    mixed = conv_weight[0] * ext[2:] + conv_weight[1] * ext[1:-1] + conv_weight[2] * ext[:-2]
    mg = swap_y(by_group(mixed)).reshape(TS, 128)
    cot_all = swap_y(head_groups(cotangent[0])).reshape(TS, HG * V)
    x_cols = jnp.transpose(
        local_x.reshape(T, NZ, NY, T), (2, 0, 1, 3)
    ).reshape(NY, T, NZ * T).astype(f32)
    x_all = swap_y(x_cols).reshape(TS, NZ * T)
    (x_flip,) = run(transpose_kernel, [((NZ * T, TS), bf16)], x_all)

    uq, uk, tot, rs = run(
        prepare_kernel,
        [((HG, TS, 128), bf16), ((HG, TS, 128), bf16), ((8, EP), f32), ((TS, 128), f32)],
        mg, sel_k, w,
    )
    etot = totals_scan(tot, 1)
    state, vb = run(
        state_kernel, [((HG * E, V), f32), ((TS, HG * V), bf16)], uk, v_all, sel_k, w
    )
    carried = state_scan(state, 1)
    dn, inv, gs = run(
        denom_kernel,
        [((TS, HG * V), bf16), ((TS, 128), f32), ((HG * E, V), f32)],
        uq, rs, etot, cot_all, sel_q, w,
    )
    gcar = state_scan(gs, -1)
    out, dq, gv_in, dk, gtot = run(
        local_kernel,
        [
            ((TS, HG * V), f32),
            ((TS, 128), f32),
            ((TS, HG * V), f32),
            ((TS, 128), f32),
            ((8, EP), f32),
        ],
        uq, uk, vb, dn, inv, etot, carried, sel_q, w,
        scratch=[pltpu.VMEM((TS, 128), f32)],
    )

    def token_rows(a):
        back = swap_y(a.reshape(NY, T, HG * V))
        return run(rows_kernel, [((T, H * V), bf16)], back)[0][None]

    mixed_out = token_rows(out)
    egtot = totals_scan(gtot, -1)
    gv, gm = run(
        key_kernel, [((TS, HG * V), f32), ((TS, 128), f32)],
        uk, vb, gv_in, dq, dk, gcar, egtot, sel_k,
    )
    grad_values = token_rows(gv)
    blocks = [gm] + [shift(gm, "y", s) for s in (1, 2, 3)]
    edge = gm[:8]
    halos = [
        lax.ppermute(
            edge, ("z", "y"),
            [((k + 1) * NY + j, k * NY + (j + s) % NY) for k in range(NZ - 1) for j in range(NY)],
        )
        for s in range(NY)
    ]
    cw = by_group(conv_weight)
    cw = jnp.transpose(cw, (1, 0, 2)).reshape(conv_weight.shape[0], 512)
    smem = pl.BlockSpec(memory_space=pltpu.SMEM)
    vm = pl.BlockSpec(memory_space=pltpu.VMEM)
    gp = pl.pallas_call(
        conv_kernel,
        out_shape=jax.ShapeDtypeStruct((TS, 512), bf16),
        in_specs=[smem] + [vm] * 9,
        out_specs=vm,
        scratch_shapes=[pltpu.VMEM((TS + 8, 128), f32)],
        compiler_params=pltpu.CompilerParams(vmem_limit_bytes=24 << 20),
    )(y.astype(jnp.int32).reshape(1), *blocks, *halos, cw)

    partial = mm(x_flip, gp).reshape(NZ, NC, NX, 16, 512)
    half = lax.dynamic_index_in_dim(partial, core, 1, False)
    other = lax.dynamic_index_in_dim(partial, 1 - core, 1, False)
    half = half + shift(other, "core", 1)

    def reduced(a, axis, me, dim):
        n = lax.axis_size(axis)
        got = lax.dynamic_index_in_dim(a, me, dim, False)
        for s in range(1, n):
            got = got + shift(
                lax.dynamic_index_in_dim(a, lax.rem(me + s, n), dim, False), axis, s
            )
        return got

    part = reduced(half, "x", x, 1)
    part = reduced(part, "z", z, 0)
    weight_rows = jnp.zeros((NC, NX, 16, 512), f32)
    mine = jnp.zeros((NX, 16, 512), f32)
    mine = lax.dynamic_update_index_in_dim(mine, part, x, 0)
    for s in (1, 2, 3):
        mine = lax.dynamic_update_index_in_dim(
            mine, shift(part, "x", s), lax.rem(x - s + NX, NX), 0
        )
    weight_rows = lax.dynamic_update_index_in_dim(weight_rows, mine, core, 0)
    weight_rows = lax.dynamic_update_index_in_dim(
        weight_rows, shift(mine, "core", 1), 1 - core, 0
    )
    weight_grad = jnp.transpose(
        weight_rows.reshape(T, NY, 2, 64), (0, 2, 1, 3)
    ).reshape(T, 512)

    own = lax.dynamic_slice_in_dim(gp, y * T, T, 0)
    own = jnp.transpose(own.reshape(T, NY, 2, 64), (0, 2, 1, 3)).reshape(T, 512)
    grad_x = mm_nt(own, qk_weight).astype(bf16)
    return (mixed_out, grad_x[None], grad_values, weight_grad)


def solution(mesh):
    inner = Mesh(mesh.devices.reshape(NX, NC, NZ, NY), ("x", "core", "z", "y"))
    rows = P(("x", "core"), ("z", "y"), None)
    return jax.shard_map(
        on_device,
        mesh=inner,
        in_specs=(rows, P(), P(), rows, rows),
        out_specs=(rows, rows, rows, P(("z", "y"), None)),
        check_vma=False,
    )
```

```python
import jax
import jax.numpy as jnp
import numpy as np
from jax import lax
from jax.experimental import pallas as pl
from jax.experimental.pallas import tpu as pltpu
from jax.sharding import Mesh, PartitionSpec as P

H = 16
F = 16
V = 128
NX, NC, NZ, NY = 4, 2, 8, 4
T = 128
TS = T * NY
HG = H // NY
E = 160
EP = 256
f32 = jnp.float32
bf16 = jnp.bfloat16


def feature_tables():
    first = np.zeros((128, 512), np.float32)
    weight = np.zeros((8, EP), np.float32)
    for f in range(128):
        i, d = f % 16, f // 16
        first[i, f] = 1
        first[(i + d) % 16, 128 + f] = 1
        weight[:, f] = 1 / 32 if d == 0 else 1 / 16
    for f in range(8):
        first[f, 256 + f] = 1
        first[f + 8, 384 + f] = 1
        weight[:, 128 + f] = 1 / 16
    for f in range(16):
        first[f, 256 + 8 + f] = 1
        first[16, 384 + 8 + f] = 0.5
        weight[:, 128 + 8 + f] = 1 / 4
    first[16, 256 + 24] = 0.5
    first[16, 384 + 24] = 0.5
    weight[:, 128 + 24] = 1
    sel_q = first.copy()
    sel_q[64:80] = first[:16]
    sel_k = first.copy()
    sel_k[32:48] = first[:16]
    return sel_q, sel_k, weight


SEL_Q, SEL_K, WEIGHT = feature_tables()
BIT_REVERSED = (0, 4, 2, 6, 1, 5, 3, 7)


def mm(a, b):
    return lax.dot_general(a, b, (((1,), (0,)), ((), ())), preferred_element_type=f32)


def mm_nt(a, b):
    return lax.dot_general(a, b, (((1,), (1,)), ((), ())), preferred_element_type=f32)


def mm_tn(a, b):
    return lax.dot_general(a, b, (((0,), (0,)), ((), ())), preferred_element_type=f32)


def run(kernel, outs, *args, scratch=(), smem=0, us=0.5):
    vm = pl.BlockSpec(memory_space=pltpu.VMEM)
    sm = pl.BlockSpec(memory_space=pltpu.SMEM)
    return pl.pallas_call(
        kernel,
        out_shape=[jax.ShapeDtypeStruct(s, d) for s, d in outs],
        in_specs=[sm] * smem + [vm] * (len(args) - smem),
        out_specs=[vm] * len(outs),
        scratch_shapes=list(scratch),
        compiler_params=pltpu.CompilerParams(vmem_limit_bytes=12 << 20),
        cost_estimate=pl.CostEstimate(
            flops=0, bytes_accessed=int(us * 3.5e6), transcendentals=0
        ),
    )(*args)


def timed(us, *args, **kwargs):
    return run(*args, us=us, **kwargs)


def features(u, sel):
    x = mm(u, sel)
    return jnp.concatenate([x[:, :128] * x[:, 128:256], x[:, 256:384] * x[:, 384:]], 1)


def feature_grad(u, sel, grad):
    x = mm(u, sel)
    g1, g2 = grad[:, :128], grad[:, 128:]
    stacked = jnp.concatenate(
        [g1 * x[:, 128:256], g1 * x[:, :128], g2 * x[:, 384:], g2 * x[:, 256:384]], 1
    ).astype(bf16)
    return mm_nt(stacked, sel)


def causal(rows, r):
    row = lax.broadcasted_iota(jnp.int32, (T, rows), 0) + r * T
    col = lax.broadcasted_iota(jnp.int32, (T, rows), 1)
    return row >= col


def lanes(h):
    return pl.ds(pl.multiple_of(h * V, V), V)


def turned(y, s):
    return lax.rem(y[0] + (s + NY), NY)


def group_lanes(g, width):
    return pl.ds(pl.multiple_of(g * width, width), width)


def pack_kernel(y, a, *outs):
    for s, o in enumerate(outs):
        o[...] = a[:, group_lanes(turned(y, s), HG * V)].astype(f32)


def after(value, *others):
    return lax.optimization_barrier((value, *others))[0]


def pack_columns_kernel(y, a, *outs):
    for s, o in enumerate(outs):
        for k in range(NZ):
            o[:, k * T : (k + 1) * T] = a[:, group_lanes(turned(y, s) + k * NY, T)].astype(f32)


def flip_kernel(y, a0, a1, a2, a3, flipped):
    for s, a in enumerate((a0, a1, a2, a3)):
        cols = group_lanes(turned(y, -s), T)
        for k in range(NZ):
            t = jnp.transpose(a[:, k * T : (k + 1) * T]).astype(bf16)
            for part in range(NC * NX):
                at = part * T + BIT_REVERSED[k] * 16
                flipped[at : at + 16, cols] = t[part * 16 : part * 16 + 16]


def mix_kernel(y, projected, halo, cw, o0, o1, o2, o3, pad, blocks):
    pad[:8] = halo[...]
    pad[8:] = projected[...]
    m = projected[...] * cw[0:1]
    for j in (1, 2):
        m += pad[8 - j : 8 - j + T] * cw[j : j + 1]
    lane = lax.broadcasted_iota(jnp.int32, (T, 128), 1)
    for g in range(NY):
        at = (g // 2) * 128
        q, k = m[:, at : at + 128], m[:, 256 + at : 256 + at + 128]
        if g % 2:
            q = pltpu.roll(q, 64, 1)
        else:
            k = pltpu.roll(k, 64, 1)
        blocks[g] = jnp.where(lane < 64, q, k)
    for s, o in enumerate((o0, o1, o2, o3)):
        o[...] = blocks[turned(y, s)]


def prepare_kernel(y, b0, b1, b2, b3, sel_k, w, uq, uk, tot, mg):
    for s, b in enumerate((b0, b1, b2, b3)):
        mg[group_lanes(turned(y, -s), T)] = b[...]
    lane = lax.broadcasted_iota(jnp.int32, (TS, 128), 1)
    tot[...] = jnp.zeros_like(tot)

    def one(h, _):
        for is_key in (0, 1):
            x = pltpu.roll(mg[...], (256 - 64 * is_key) - 16 * h, 1)
            hi = x.astype(bf16).astype(f32)
            lo = x - hi
            a, b = (lo, hi) if is_key else (hi, lo)
            u = jnp.where(lane < 16, hi, jnp.where(lane == 16, 2.0, 0.0))
            u = jnp.where((lane >= 32) & (lane < 48), pltpu.roll(a, 32, 1), u)
            u = jnp.where((lane >= 64) & (lane < 80), pltpu.roll(b, 64, 1), u)
            (uk if is_key else uq)[h] = u.astype(bf16)
        rk = features(uk[h], sel_k[...])
        tot[pl.ds(h, 1)] = jnp.sum(rk, 0, keepdims=True) * w[0:1]
        return 0

    lax.fori_loop(0, HG, one, 0)


def halves(scratch, p, keep, send):
    keep[...] = scratch[p]
    send[...] = scratch[1 - p]


def state_kernel(p, y, uq, uk, v0, v1, v2, v3, sel_k, w, keep, send, vb, rs, scratch):
    for s, v in enumerate((v0, v1, v2, v3)):
        vb[group_lanes(turned(y, -s), T)] = v[...].astype(bf16)

    def one(h, _):
        rk = (features(uk[h], sel_k[...]) * w[0:1]).astype(bf16)
        s = mm_tn(rk, vb[:, lanes(h)])
        scratch[lax.div(h, 2), pl.ds(pl.multiple_of(lax.rem(h, 2) * E, E), E)] = s[:E]
        for r in range(NY):
            rows = (r + 1) * T
            t = mm_nt(uq[h, r * T : rows], uk[h, :rows])
            t = jnp.where(causal(rows, r), 0.5 + t * t * (1 / 32), 0.0)
            rs[h, r * T : rows] = jnp.broadcast_to(jnp.sum(t, 1, keepdims=True), (T, V))
        return 0

    lax.fori_loop(0, HG, one, 0)
    halves(scratch, p[0], keep, send)


def denom_kernel(p, y, uq, rs, etot, c0, c1, c2, c3, sel_q, w, keep, send, dn, inv, scratch):
    def one(h, _):
        rq = features(uq[h], sel_q[...])
        den = rs[h] + jnp.sum(rq * etot[pl.ds(h, 1)], 1, keepdims=True)
        iv = 1.0 / den
        inv[h] = iv
        for s, c in enumerate((c0, c1, c2, c3)):
            rows = group_lanes(turned(y, -s), T)
            dn[rows, lanes(h)] = (c[:, lanes(h)] * inv[h, rows]).astype(bf16)
        s = mm_tn((rq * w[0:1]).astype(bf16), dn[:, lanes(h)])
        scratch[lax.div(h, 2), pl.ds(pl.multiple_of(lax.rem(h, 2) * E, E), E)] = s[:E]
        return 0

    lax.fori_loop(0, HG, one, 0)
    halves(scratch, p[0], keep, send)


def pair_kernel(use, keep, got, e0, e1, e2, own, partner):
    base = e0[...] + e1[...] + e2[...]
    own[...] = base + jnp.where(use[0] > 0, got[...], 0.0)
    partner[...] = base + jnp.where(use[0] > 0, 0.0, keep[...])


def fill_states(p, own, got, scratch):
    zero = jnp.zeros((EP - E, V), bf16)
    for which, a in ((p, own), (1 - p, got)):
        for i in range(2):
            scratch[2 * which + i, :E] = a[i * E : (i + 1) * E].astype(bf16)
            scratch[2 * which + i, E:] = zero


def local_kernel(
    p, y, uq, uk, vb, dn, inv, etot, own, got, sel_q, w,
    o0, o1, o2, o3, dq, gv, dk, gtot, dk_acc, states, out,
):
    lane = lax.broadcasted_iota(jnp.int32, (TS, 128), 1)
    gtot[...] = jnp.zeros_like(gtot)
    dq[...] = jnp.zeros_like(dq)
    dk[...] = jnp.zeros_like(dk)
    fill_states(p[0], own, got, states)

    def one(h, _):
        cols = lanes(h)
        c = states[h]
        tot_row = etot[pl.ds(h, 1)]
        gsum = jnp.zeros((1, EP), f32)
        grads = []
        for r in reversed(range(NY)):
            rows = (r + 1) * T
            mine = slice(r * T, rows)
            u = uq[h, mine]
            keep = causal(rows, r)
            s = mm_nt(u, uk[h, :rows])
            pr = jnp.where(keep, 0.5 + s * s * (1 / 32), 0.0).astype(bf16)
            rq = features(u, sel_q[...])
            numer = mm(pr, vb[:rows, cols]) + mm(rq.astype(bf16), c)
            o = numer * inv[h, mine]
            out[r, :, cols] = o
            d = dn[mine, cols]
            dd = -jnp.sum(d.astype(f32) * o, 1, keepdims=True)
            dp = mm_nt(d, vb[:rows, cols]) + dd
            ds = jnp.where(keep, dp * s * (1 / 16), 0.0).astype(bf16)
            gsum += jnp.sum(rq * dd, 0, keepdims=True)
            dr = mm_nt(d, c) + dd * tot_row
            grads.append(mm(ds, uk[h, :rows]) + feature_grad(u, sel_q[...], dr))
            gv_add = mm_tn(pr, d)
            dk_add = mm_tn(ds, u)
            if r == NY - 1:
                gv[:, cols] = gv_add
                dk_acc[...] = dk_add
            else:
                gv[:rows, cols] += gv_add
                dk_acc[:rows] += dk_add
        gtot[pl.ds(h, 1)] = gsum * w[0:1]
        g = jnp.concatenate(grads[::-1], 0)
        dq[...] += pltpu.roll(jnp.where(lane < 16, g, 0.0), 16 * h, 1)
        dk[...] += pltpu.roll(jnp.where(lane < 16, dk_acc[...], 0.0), 64 + 16 * h, 1)
        return 0

    lax.fori_loop(0, HG, one, 0)
    for s, o in enumerate((o0, o1, o2, o3)):
        o[...] = out[turned(y, s)]


def key_kernel(
    p, y, uk, vb, gv_in, dq, dk, own, got, egtot, sel_k,
    o0, o1, o2, o3, gm, edge, states, gv,
):
    lane = lax.broadcasted_iota(jnp.int32, (TS, 128), 1)
    fill_states(p[0], own, got, states)
    gm[...] = dq[...] + dk[...]

    def one(h, _):
        cols = lanes(h)
        c = states[h]
        rk = features(uk[h], sel_k[...]).astype(bf16)
        gv[:, cols] = gv_in[:, cols] + mm(rk, c)
        dr = mm_nt(vb[:, cols], c) + egtot[pl.ds(h, 1)]
        g = feature_grad(uk[h], sel_k[...], dr)
        gm[...] += pltpu.roll(jnp.where(lane < 16, g, 0.0), 64 + 16 * h, 1)
        return 0

    lax.fori_loop(0, HG, one, 0)
    edge[...] = gm[:8]
    for s, o in enumerate((o0, o1, o2, o3)):
        o[...] = gv[group_lanes(turned(y, s), T)]


def conv_back_kernel(y, gm, halo, cw, gp, pad):
    pad[:TS] = gm[...]
    pad[TS:] = halo[...]
    cols = group_lanes(y[0], 128)
    total = gm[...] * cw[0:1, cols]
    for j in (1, 2):
        total += pad[j : TS + j] * cw[j : j + 1, cols]
    gp[...] = total


def weight_kernel(at, g0, g1, g2, g3, flipped, keep, send, grad_own, gp):
    y, core = at[0], at[1]
    for s, g in enumerate((g0, g1, g2, g3)):
        gp[:, group_lanes(turned(at, -s), 128)] = g[...].astype(bf16)
    half = NZ * T // 2
    for which, ref in ((1 - core, send), (core, keep)):
        ref[...] = mm(flipped[group_lanes(which, half)], gp[...])
    grad_own[...] = gp[group_lanes(y, T)]


def split_x_kernel(x, a, b, o0, o1, o2, o3):
    for s, o in enumerate((o0, o1, o2, o3)):
        rows = pl.ds(pl.multiple_of(lax.rem(x[0] + s, NX) * T, T), T)
        o[...] = a[rows] + b[rows]


def split_z_kernel(bit, *refs):
    ins, (keep, send) = refs[:-2], refs[-2:]
    n = keep.shape[0]
    for which, o in ((bit[0], keep), (1 - bit[0], send)):
        rows = pl.ds(pl.multiple_of(which * n, n), n)
        total = ins[0][rows]
        for a in ins[1:]:
            total += a[rows]
        o[...] = total


def stack_kernel(core, a, b, c, d, o):
    total = a[...] + b[...]
    o[group_lanes(core[0], 16)] = total
    o[group_lanes(1 - core[0], 16)] = c[...] + d[...]


def finish_kernel(x, m0, m1, m2, m3, rows):
    lane = lax.broadcasted_iota(jnp.int32, (16, 128), 1)
    for s, m in enumerate((m0, m1, m2, m3)):
        src = lax.rem(x[0] - s + NX, NX)
        for core in range(NC):
            at = pl.ds(pl.multiple_of(core * 64 + src * 16, 16), 16)
            b = m[core * 16 : core * 16 + 16]
            for half in range(2):
                lo, hi = b[:, half * 256 : half * 256 + 128], b[:, half * 256 + 128 : half * 256 + 256]
                q = jnp.where(lane < 64, lo, pltpu.roll(hi, 64, 1))
                k = jnp.where(lane < 64, pltpu.roll(lo, 64, 1), hi)
                rows[at, half * 128 : half * 128 + 128] = q
                rows[at, 256 + half * 128 : 256 + half * 128 + 128] = k


def rows_kernel(y, b0, b1, b2, b3, rows):
    for s, b in enumerate((b0, b1, b2, b3)):
        rows[:, group_lanes(turned(y, -s), HG * V)] = b[...].astype(bf16)


def shift(value, axis, by):
    n = lax.axis_size(axis)
    return lax.ppermute(value, axis, [(i, (i + by) % n) for i in range(n)])


def shift_open(value, axis, by):
    n = lax.axis_size(axis)
    return lax.ppermute(
        value, axis, [(i, i + by) for i in range(n) if 0 <= i + by < n]
    )


def swap(value, axis, mask):
    n = lax.axis_size(axis)
    return lax.ppermute(value, axis, [(i, i ^ mask) for i in range(n)])


def totals_scan(tot, sign):
    near = sum(shift_open(tot, "z", sign * s) for s in (1, 2, 3))
    far = shift_open(near + tot, "z", sign * 4)
    return near + far


def across_pairs(keep, got, sign):
    total = keep + got
    return [shift_open(total, "z", sign * d) for d in (2, 4, 6)]


def back_to_pair(keep, got, others, use):
    half = ((2 * E, V), f32)
    own, partner = run(pair_kernel, [half, half], use, keep, got, *others, smem=1)
    return own, swap(partner, "z", 1)


def swap_y(blocks):
    return [blocks[0]] + [shift(blocks[s], "y", s) for s in (1, 2, 3)]


def on_device(tokens, qk_weight, conv_weight, values, cotangent):
    def place(name):
        return lax.axis_index(name).astype(jnp.int32)

    x, core, z, y = place("x"), place("core"), place("z"), place("y")
    y1, parity = y.reshape(1), lax.rem(z, 2).reshape(1)
    sel_q, sel_k = jnp.asarray(SEL_Q, bf16), jnp.asarray(SEL_K, bf16)
    w = jnp.asarray(WEIGHT, f32)
    local_x = tokens[0]
    wide = HG * V

    projected = jnp.dot(local_x, qk_weight, preferred_element_type=f32)
    halo = lax.ppermute(
        projected[T - 8 :], ("z", "y"), [(i, i + 1) for i in range(NZ * NY - 1)]
    )
    by_head = [((T, wide), f32)] * NY
    v_packed = run(pack_kernel, by_head, y1, after(values[0], projected), smem=1)
    c_packed = run(pack_kernel, by_head, y1, after(cotangent[0], projected), smem=1)
    mixed = run(
        mix_kernel, [((T, 128), f32)] * NY, y1, projected, halo, conv_weight, smem=1,
        scratch=[pltpu.VMEM((T + 8, 512), f32), pltpu.VMEM((NY, T, 128), f32)],
    )
    mixed = swap_y(mixed)
    v_all = swap_y(lax.optimization_barrier((*v_packed, *mixed))[:NY])
    uq, uk, tot = timed(
        2.6, prepare_kernel,
        [((HG, TS, 128), bf16), ((HG, TS, 128), bf16), ((8, EP), f32)],
        y1, *mixed, sel_k, w, smem=1, scratch=[pltpu.VMEM((TS, 128), f32)],
    )
    c_all = swap_y(lax.optimization_barrier((*c_packed, tot))[:NY])
    etot = totals_scan(tot, 1)
    half = ((2 * E, V), f32)
    half_scratch = [pltpu.VMEM((2, 2 * E, V), f32)]
    keep, send, vb, rs = timed(
        2.8, state_kernel, [half, half, ((TS, wide), bf16), ((HG, TS, V), f32)],
        parity, y1, uq, uk, *v_all, sel_k, w, smem=2, scratch=half_scratch,
    )
    g_keep, g_send, dn, inv = timed(
        2.4, denom_kernel, [half, half, ((TS, wide), bf16), ((HG, TS, V), f32)],
        parity, y1, uq, rs, etot, *c_all, sel_q, w, smem=2, scratch=half_scratch,
    )
    pair = swap(after(send, etot), "z", 1)
    g_pair = swap(g_send, "z", 1)
    earlier = across_pairs(keep, pair, 1)
    g_later = across_pairs(g_keep, g_pair, -1)
    own, got = back_to_pair(keep, after(pair, g_pair), earlier, parity)
    own = after(own, *g_later)
    g_own, g_got = back_to_pair(g_keep, g_pair, g_later, 1 - parity)

    x_packed = timed(
        1.5, pack_columns_kernel, [((T, NZ * T), f32)] * NY, y1, after(local_x, g_keep), smem=1
    )
    (flipped,) = timed(
        1.9, flip_kernel, [((NZ * T, TS), bf16)], y1, *swap_y(x_packed), smem=1
    )

    states = pltpu.VMEM((HG, EP, V), bf16)
    square = ((TS, 128), f32)
    *out, dq, gv_in, dk, gtot = timed(
        9.5, local_kernel,
        by_head + [square, ((TS, wide), f32), square, ((8, EP), f32)],
        parity, y1, uq, uk, vb, dn, inv, etot, own, got, sel_q, w, smem=2,
        scratch=[pltpu.VMEM((TS, 128), f32), states, pltpu.VMEM((NY, T, wide), f32)],
    )
    egtot = totals_scan(gtot, -1)

    def token_rows(blocks):
        return run(rows_kernel, [((T, H * V), bf16)], y1, *swap_y(blocks), smem=1)[0]

    mixed_out = token_rows(out)
    egtot = after(egtot, flipped)
    *gv, gm, edge = timed(
        3.5, key_kernel, by_head + [square, ((8, 128), f32)],
        parity, y1, uk, vb, gv_in, dq, dk, g_own, g_got, egtot, sel_k, smem=2,
        scratch=[states, pltpu.VMEM((TS, wide), f32)],
    )
    taps = conv_weight.shape[0]
    cw = jnp.transpose(conv_weight.reshape(taps, 2, NY, 64), (0, 2, 1, 3)).reshape(taps, 512)
    (gp,) = run(
        conv_back_kernel, [square], y1, after(gm, mixed_out), shift_open(edge, "z", -1), cw, smem=1,
        scratch=[pltpu.VMEM((TS + 8, 128), f32)],
    )
    blocks = [gp] + [shift(gp, "y", s) for s in (1, 2, 3)]
    keep, send, grad_own = timed(
        2.0, weight_kernel,
        [((NZ * T // 2, 512), f32), ((NZ * T // 2, 512), f32), ((T, 512), bf16)],
        jnp.stack([y, core]), *blocks, flipped, smem=1,
        scratch=[pltpu.VMEM((TS, 512), bf16)],
    )
    quarter = ((T, 512), f32)
    parts = run(
        split_x_kernel, [quarter] * NX, x.reshape(1), keep, swap(send, "core", 1), smem=1
    )
    own_rows = jnp.transpose(
        after(grad_own, parts[0]).reshape(T, NY, 2, 64), (0, 2, 1, 3)
    ).reshape(T, 512)
    grad_x = mm_nt(own_rows, qk_weight).astype(bf16)
    grad_values = token_rows(lax.optimization_barrier((*gv, parts[0]))[:NY])
    parts = [parts[0]] + [shift(parts[s], "x", s) for s in (1, 2, 3)]
    parts[0] = after(parts[0], grad_x, grad_values)
    for mask in (1, 2, 4):
        n = 64 // mask
        bit = lax.rem(lax.div(z, mask), 2).reshape(1)
        keep, send = run(
            split_z_kernel, [((n, 512), f32), ((n, 512), f32)], bit, *parts, smem=1
        )
        parts = [keep, swap(send, "z", mask)]
    (pair_rows,) = run(
        stack_kernel, [((32, 512), f32)], core.reshape(1), *parts,
        *[swap(a, "core", 1) for a in parts], smem=1,
    )
    stacks = [pair_rows] + [shift(pair_rows, "x", s) for s in (1, 2, 3)]
    (weight_grad,) = run(finish_kernel, [((T, 512), f32)], x.reshape(1), *stacks, smem=1)

    return (mixed_out[None], grad_x[None], grad_values[None], weight_grad)


def solution(mesh):
    inner = Mesh(mesh.devices.reshape(NX, NC, NZ, NY), ("x", "core", "z", "y"))
    rows = P(("x", "core"), ("z", "y"), None)
    return jax.shard_map(
        on_device,
        mesh=inner,
        in_specs=(rows, P(), P(), rows, rows),
        out_specs=(rows, rows, rows, P(("z", "y"), None)),
        check_vma=False,
    )
```

```python
import jax
import jax.numpy as jnp
import numpy as np
from jax import lax
from jax.experimental import pallas as pl
from jax.experimental.pallas import tpu as pltpu
from jax.sharding import Mesh, PartitionSpec as P

H = 16
F = 16
V = 128
NX, NC, NZ, NY = 4, 2, 8, 4
T = 128
TS = T * NY
HG = H // NY
E = 160
EP = 256
f32 = jnp.float32
bf16 = jnp.bfloat16


def feature_tables():
    first = np.zeros((128, 512), np.float32)
    weight = np.zeros((8, EP), np.float32)
    for f in range(128):
        i, d = f % 16, f // 16
        first[i, f] = 1
        first[(i + d) % 16, 128 + f] = 1
        weight[:, f] = 1 / 32 if d == 0 else 1 / 16
    for f in range(8):
        first[f, 256 + f] = 1
        first[f + 8, 384 + f] = 1
        weight[:, 128 + f] = 1 / 16
    for f in range(16):
        first[f, 256 + 8 + f] = 1
        first[16, 384 + 8 + f] = 0.5
        weight[:, 128 + 8 + f] = 1 / 4
    first[16, 256 + 24] = 0.5
    first[16, 384 + 24] = 0.5
    weight[:, 128 + 24] = 1
    sel_q = first.copy()
    sel_q[64:80] = first[:16]
    sel_k = first.copy()
    sel_k[32:48] = first[:16]
    return sel_q, sel_k, weight


SEL_Q, SEL_K, WEIGHT = feature_tables()
BIT_REVERSED = (0, 4, 2, 6, 1, 5, 3, 7)


def mm(a, b):
    return lax.dot_general(a, b, (((1,), (0,)), ((), ())), preferred_element_type=f32)


def mm_nt(a, b):
    return lax.dot_general(a, b, (((1,), (1,)), ((), ())), preferred_element_type=f32)


def mm_tn(a, b):
    return lax.dot_general(a, b, (((0,), (0,)), ((), ())), preferred_element_type=f32)


def run(kernel, outs, *args, scratch=(), smem=0, us=0.5):
    vm = pl.BlockSpec(memory_space=pltpu.VMEM)
    sm = pl.BlockSpec(memory_space=pltpu.SMEM)
    return pl.pallas_call(
        kernel,
        out_shape=[jax.ShapeDtypeStruct(s, d) for s, d in outs],
        in_specs=[sm] * smem + [vm] * (len(args) - smem),
        out_specs=[vm] * len(outs),
        scratch_shapes=list(scratch),
        compiler_params=pltpu.CompilerParams(vmem_limit_bytes=12 << 20),
        cost_estimate=pl.CostEstimate(
            flops=0, bytes_accessed=int(us * 3.5e6), transcendentals=0
        ),
    )(*args)


def timed(us, *args, **kwargs):
    return run(*args, us=us, **kwargs)


def features(u, sel):
    x = mm(u, sel)
    return jnp.concatenate([x[:, :128] * x[:, 128:256], x[:, 256:384] * x[:, 384:]], 1)


def feature_grad(u, sel, grad):
    x = mm(u, sel)
    g1, g2 = grad[:, :128], grad[:, 128:]
    stacked = jnp.concatenate(
        [g1 * x[:, 128:256], g1 * x[:, :128], g2 * x[:, 384:], g2 * x[:, 256:384]], 1
    ).astype(bf16)
    return mm_nt(stacked, sel)


def causal(rows, r):
    row = lax.broadcasted_iota(jnp.int32, (T, rows), 0) + r * T
    col = lax.broadcasted_iota(jnp.int32, (T, rows), 1)
    return row >= col


def lanes(h):
    return pl.ds(pl.multiple_of(h * V, V), V)


def turned(y, s):
    return lax.rem(y[0] + (s + NY), NY)


def group_lanes(g, width):
    return pl.ds(pl.multiple_of(g * width, width), width)


def pack_kernel(y, a, *outs):
    for s, o in enumerate(outs):
        o[...] = a[:, group_lanes(turned(y, s), HG * V)].astype(f32)


def after(value, *others):
    return lax.optimization_barrier((value, *others))[0]


def pack_columns_kernel(y, a, *outs):
    for s, o in enumerate(outs):
        for k in range(NZ):
            o[:, k * T : (k + 1) * T] = a[:, group_lanes(turned(y, s) + k * NY, T)].astype(f32)


def flip_kernel(y, a0, a1, a2, a3, flipped):
    for s, a in enumerate((a0, a1, a2, a3)):
        cols = group_lanes(turned(y, -s), T)
        for k in range(NZ):
            t = jnp.transpose(a[:, k * T : (k + 1) * T]).astype(bf16)
            for part in range(NC * NX):
                at = part * T + BIT_REVERSED[k] * 16
                flipped[at : at + 16, cols] = t[part * 16 : part * 16 + 16]


def mix_kernel(y, projected, halo, cw, o0, o1, o2, o3, pad, blocks):
    pad[:8] = halo[...]
    pad[8:] = projected[...]
    m = projected[...] * cw[0:1]
    for j in (1, 2):
        m += pad[8 - j : 8 - j + T] * cw[j : j + 1]
    lane = lax.broadcasted_iota(jnp.int32, (T, 128), 1)
    for g in range(NY):
        at = (g // 2) * 128
        q, k = m[:, at : at + 128], m[:, 256 + at : 256 + at + 128]
        if g % 2:
            q = pltpu.roll(q, 64, 1)
        else:
            k = pltpu.roll(k, 64, 1)
        blocks[g] = jnp.where(lane < 64, q, k)
    for s, o in enumerate((o0, o1, o2, o3)):
        o[...] = blocks[turned(y, s)]


def prepare_kernel(y, b0, b1, b2, b3, sel_k, w, uq, uk, tot, mg):
    for s, b in enumerate((b0, b1, b2, b3)):
        mg[group_lanes(turned(y, -s), T)] = b[...]
    lane = lax.broadcasted_iota(jnp.int32, (TS, 128), 1)
    tot[...] = jnp.zeros_like(tot)

    def one(h, _):
        for is_key in (0, 1):
            x = pltpu.roll(mg[...], (256 - 64 * is_key) - 16 * h, 1)
            hi = x.astype(bf16).astype(f32)
            lo = x - hi
            a, b = (lo, hi) if is_key else (hi, lo)
            u = jnp.where(lane < 16, hi, jnp.where(lane == 16, 2.0, 0.0))
            u = jnp.where((lane >= 32) & (lane < 48), pltpu.roll(a, 32, 1), u)
            u = jnp.where((lane >= 64) & (lane < 80), pltpu.roll(b, 64, 1), u)
            (uk if is_key else uq)[h] = u.astype(bf16)
        rk = features(uk[h], sel_k[...])
        tot[pl.ds(h, 1)] = jnp.sum(rk, 0, keepdims=True) * w[0:1]
        return 0

    lax.fori_loop(0, HG, one, 0)


def halves(scratch, p, keep, send):
    keep[...] = scratch[p]
    send[...] = scratch[1 - p]


def state_kernel(p, y, uq, uk, v0, v1, v2, v3, sel_k, w, keep, send, vb, rs, scratch):
    for s, v in enumerate((v0, v1, v2, v3)):
        vb[group_lanes(turned(y, -s), T)] = v[...].astype(bf16)

    def one(h, _):
        rk = (features(uk[h], sel_k[...]) * w[0:1]).astype(bf16)
        s = mm_tn(rk, vb[:, lanes(h)])
        scratch[lax.div(h, 2), pl.ds(pl.multiple_of(lax.rem(h, 2) * E, E), E)] = s[:E]
        for r in range(NY):
            rows = (r + 1) * T
            t = mm_nt(uq[h, r * T : rows], uk[h, :rows])
            t = jnp.where(causal(rows, r), 0.5 + t * t * (1 / 32), 0.0)
            rs[h, r * T : rows] = jnp.broadcast_to(jnp.sum(t, 1, keepdims=True), (T, V))
        return 0

    lax.fori_loop(0, HG, one, 0)
    halves(scratch, p[0], keep, send)


def denom_kernel(p, y, uq, rs, etot, c0, c1, c2, c3, sel_q, w, keep, send, dn, inv, scratch):
    def one(h, _):
        rq = features(uq[h], sel_q[...])
        den = rs[h] + jnp.sum(rq * etot[pl.ds(h, 1)], 1, keepdims=True)
        iv = 1.0 / den
        inv[h] = iv
        for s, c in enumerate((c0, c1, c2, c3)):
            rows = group_lanes(turned(y, -s), T)
            dn[rows, lanes(h)] = (c[:, lanes(h)] * inv[h, rows]).astype(bf16)
        s = mm_tn((rq * w[0:1]).astype(bf16), dn[:, lanes(h)])
        scratch[lax.div(h, 2), pl.ds(pl.multiple_of(lax.rem(h, 2) * E, E), E)] = s[:E]
        return 0

    lax.fori_loop(0, HG, one, 0)
    halves(scratch, p[0], keep, send)


def pair_kernel(use, keep, got, e0, e1, e2, own, partner):
    base = e0[...] + e1[...] + e2[...]
    own[...] = base + jnp.where(use[0] > 0, got[...], 0.0)
    partner[...] = base + jnp.where(use[0] > 0, 0.0, keep[...])


def fill_states(p, own, got, scratch):
    zero = jnp.zeros((EP - E, V), bf16)
    for which, a in ((p, own), (1 - p, got)):
        for i in range(2):
            scratch[2 * which + i, :E] = a[i * E : (i + 1) * E].astype(bf16)
            scratch[2 * which + i, E:] = zero


def local_kernel(
    p, uq, uk, vb, dn, inv, etot, own, got, sel_q, w, out, dq, gv, dk, gtot, dk_acc, states
):
    lane = lax.broadcasted_iota(jnp.int32, (TS, 128), 1)
    gtot[...] = jnp.zeros_like(gtot)
    dq[...] = jnp.zeros_like(dq)
    dk[...] = jnp.zeros_like(dk)
    fill_states(p[0], own, got, states)

    def one(h, _):
        cols = lanes(h)
        c = states[h]
        tot_row = etot[pl.ds(h, 1)]
        gsum = jnp.zeros((1, EP), f32)
        grads = []
        for r in reversed(range(NY)):
            rows = (r + 1) * T
            mine = slice(r * T, rows)
            u = uq[h, mine]
            keep = causal(rows, r)
            s = mm_nt(u, uk[h, :rows])
            pr = jnp.where(keep, 0.5 + s * s * (1 / 32), 0.0).astype(bf16)
            rq = features(u, sel_q[...])
            numer = mm(pr, vb[:rows, cols]) + mm(rq.astype(bf16), c)
            o = numer * inv[h, mine]
            out[r, :, cols] = o
            d = dn[mine, cols]
            dd = -jnp.sum(d.astype(f32) * o, 1, keepdims=True)
            dp = mm_nt(d, vb[:rows, cols]) + dd
            ds = jnp.where(keep, dp * s * (1 / 16), 0.0).astype(bf16)
            gsum += jnp.sum(rq * dd, 0, keepdims=True)
            dr = mm_nt(d, c) + dd * tot_row
            grads.append(mm(ds, uk[h, :rows]) + feature_grad(u, sel_q[...], dr))
            gv_add = mm_tn(pr, d)
            dk_add = mm_tn(ds, u)
            if r == NY - 1:
                gv[:, cols] = gv_add
                dk_acc[...] = dk_add
            else:
                gv[:rows, cols] += gv_add
                dk_acc[:rows] += dk_add
        gtot[pl.ds(h, 1)] = gsum * w[0:1]
        g = jnp.concatenate(grads[::-1], 0)
        dq[...] += pltpu.roll(jnp.where(lane < 16, g, 0.0), 16 * h, 1)
        dk[...] += pltpu.roll(jnp.where(lane < 16, dk_acc[...], 0.0), 64 + 16 * h, 1)
        return 0

    lax.fori_loop(0, HG, one, 0)


def key_kernel(
    p, y, uk, vb, gv_in, dq, dk, own, got, egtot, out, sel_k,
    o0, o1, o2, o3, gm, edge, states, gv,
):
    lane = lax.broadcasted_iota(jnp.int32, (TS, 128), 1)
    fill_states(p[0], own, got, states)
    gm[...] = dq[...] + dk[...]

    def one(h, _):
        cols = lanes(h)
        c = states[h]
        rk = features(uk[h], sel_k[...]).astype(bf16)
        gv[:, cols] = gv_in[:, cols] + mm(rk, c)
        dr = mm_nt(vb[:, cols], c) + egtot[pl.ds(h, 1)]
        g = feature_grad(uk[h], sel_k[...], dr)
        gm[...] += pltpu.roll(jnp.where(lane < 16, g, 0.0), 64 + 16 * h, 1)
        return 0

    lax.fori_loop(0, HG, one, 0)
    edge[...] = gm[:8]
    for s, o in enumerate((o0, o1, o2, o3)):
        o[:, : HG * V] = out[turned(y, s)]
        o[:, HG * V :] = gv[group_lanes(turned(y, s), T)]


def conv_back_kernel(y, gm, halo, cw, gp, pad):
    pad[:TS] = gm[...]
    pad[TS:] = halo[...]
    cols = group_lanes(y[0], 128)
    total = gm[...] * cw[0:1, cols]
    for j in (1, 2):
        total += pad[j : TS + j] * cw[j : j + 1, cols]
    gp[...] = total


def weight_kernel(at, g0, g1, g2, g3, flipped, keep, send, grad_own, gp):
    y, core = at[0], at[1]
    for s, g in enumerate((g0, g1, g2, g3)):
        gp[:, group_lanes(turned(at, -s), 128)] = g[...].astype(bf16)
    half = NZ * T // 2
    for which, ref in ((1 - core, send), (core, keep)):
        ref[...] = mm(flipped[group_lanes(which, half)], gp[...])
    grad_own[...] = gp[group_lanes(y, T)]


def split_x_kernel(x, a, b, o0, o1, o2, o3):
    for s, o in enumerate((o0, o1, o2, o3)):
        rows = pl.ds(pl.multiple_of(lax.rem(x[0] + s, NX) * T, T), T)
        o[...] = a[rows] + b[rows]


def split_z_kernel(bit, *refs):
    ins, (keep, send) = refs[:-2], refs[-2:]
    n = keep.shape[0]
    for which, o in ((bit[0], keep), (1 - bit[0], send)):
        rows = pl.ds(pl.multiple_of(which * n, n), n)
        total = ins[0][rows]
        for a in ins[1:]:
            total += a[rows]
        o[...] = total


def stack_kernel(core, a, b, c, d, o):
    total = a[...] + b[...]
    o[group_lanes(core[0], 16)] = total
    o[group_lanes(1 - core[0], 16)] = c[...] + d[...]


def finish_kernel(x, m0, m1, m2, m3, rows):
    lane = lax.broadcasted_iota(jnp.int32, (16, 128), 1)
    for s, m in enumerate((m0, m1, m2, m3)):
        src = lax.rem(x[0] - s + NX, NX)
        for core in range(NC):
            at = pl.ds(pl.multiple_of(core * 64 + src * 16, 16), 16)
            b = m[core * 16 : core * 16 + 16]
            for half in range(2):
                lo, hi = b[:, half * 256 : half * 256 + 128], b[:, half * 256 + 128 : half * 256 + 256]
                q = jnp.where(lane < 64, lo, pltpu.roll(hi, 64, 1))
                k = jnp.where(lane < 64, pltpu.roll(lo, 64, 1), hi)
                rows[at, half * 128 : half * 128 + 128] = q
                rows[at, 256 + half * 128 : 256 + half * 128 + 128] = k


def rows_kernel(y, b0, b1, b2, b3, out, grad):
    for s, b in enumerate((b0, b1, b2, b3)):
        cols = group_lanes(turned(y, -s), HG * V)
        out[:, cols] = b[:, : HG * V].astype(bf16)
        grad[:, cols] = b[:, HG * V :].astype(bf16)


def shift(value, axis, by):
    n = lax.axis_size(axis)
    return lax.ppermute(value, axis, [(i, (i + by) % n) for i in range(n)])


def shift_open(value, axis, by):
    n = lax.axis_size(axis)
    return lax.ppermute(
        value, axis, [(i, i + by) for i in range(n) if 0 <= i + by < n]
    )


def swap(value, axis, mask):
    n = lax.axis_size(axis)
    return lax.ppermute(value, axis, [(i, i ^ mask) for i in range(n)])


def totals_scan(tot, sign):
    before = shift_open(tot, "z", sign)
    before = before + shift_open(before + tot, "z", 2 * sign)
    return before + shift_open(before + tot, "z", 4 * sign)


def across_pairs(keep, got, sign):
    total = keep + got
    return [shift_open(total, "z", sign * d) for d in (2, 4, 6)]


def back_to_pair(keep, got, others, use):
    half = ((2 * E, V), f32)
    own, partner = run(pair_kernel, [half, half], use, keep, got, *others, smem=1)
    return own, swap(partner, "z", 1)


def swap_y(blocks):
    return [blocks[0]] + [shift(blocks[s], "y", s) for s in (1, 2, 3)]


def on_device(tokens, qk_weight, conv_weight, values, cotangent):
    def place(name):
        return lax.axis_index(name).astype(jnp.int32)

    x, core, z, y = place("x"), place("core"), place("z"), place("y")
    y1, parity = y.reshape(1), lax.rem(z, 2).reshape(1)
    sel_q, sel_k = jnp.asarray(SEL_Q, bf16), jnp.asarray(SEL_K, bf16)
    w = jnp.asarray(WEIGHT, f32)
    local_x = tokens[0]
    wide = HG * V

    by_head = [((T, wide), f32)] * NY
    v_all = swap_y(run(pack_kernel, by_head, y1, values[0], smem=1))
    projected = jnp.dot(local_x, qk_weight, preferred_element_type=f32)
    halo = lax.ppermute(
        projected[T - 8 :], ("z", "y"), [(i, i + 1) for i in range(NZ * NY - 1)]
    )
    c_packed = run(pack_kernel, by_head, y1, after(cotangent[0], projected), smem=1)
    mixed = run(
        mix_kernel, [((T, 128), f32)] * NY, y1, after(projected, *v_all), halo, conv_weight, smem=1,
        scratch=[pltpu.VMEM((T + 8, 512), f32), pltpu.VMEM((NY, T, 128), f32)],
    )
    mixed = swap_y(mixed)
    uq, uk, tot = timed(
        2.6, prepare_kernel,
        [((HG, TS, 128), bf16), ((HG, TS, 128), bf16), ((8, EP), f32)],
        y1, *mixed, sel_k, w, smem=1, scratch=[pltpu.VMEM((TS, 128), f32)],
    )
    c_all = swap_y(lax.optimization_barrier((*c_packed, tot))[:NY])
    etot = totals_scan(tot, 1)
    half = ((2 * E, V), f32)
    half_scratch = [pltpu.VMEM((2, 2 * E, V), f32)]
    keep, send, vb, rs = timed(
        2.8, state_kernel, [half, half, ((TS, wide), bf16), ((HG, TS, V), f32)],
        parity, y1, uq, uk, *v_all, sel_k, w, smem=2, scratch=half_scratch,
    )
    g_keep, g_send, dn, inv = timed(
        2.4, denom_kernel, [half, half, ((TS, wide), bf16), ((HG, TS, V), f32)],
        parity, y1, uq, rs, etot, *c_all, sel_q, w, smem=2, scratch=half_scratch,
    )
    pair = swap(after(send, etot), "z", 1)
    g_pair = swap(g_send, "z", 1)
    earlier = across_pairs(keep, pair, 1)
    g_later = across_pairs(g_keep, g_pair, -1)
    own, got = back_to_pair(keep, after(pair, g_pair), earlier, parity)
    g_own, g_got = back_to_pair(g_keep, g_pair, g_later, 1 - parity)

    states = pltpu.VMEM((HG, EP, V), bf16)
    square = ((TS, 128), f32)
    out, dq, gv_in, dk, gtot = timed(
        9.5, local_kernel,
        [((NY, T, wide), f32), square, ((TS, wide), f32), square, ((8, EP), f32)],
        parity, uq, uk, vb, dn, inv, etot, own, got, sel_q, w, smem=1,
        scratch=[pltpu.VMEM((TS, 128), f32), states],
    )
    x_packed = timed(
        1.5, pack_columns_kernel, [((T, NZ * T), f32)] * NY, y1, after(local_x, etot), smem=1
    )
    x_all = swap_y(lax.optimization_barrier((*x_packed, gtot))[:NY])
    (flipped,) = timed(1.9, flip_kernel, [((NZ * T, TS), bf16)], y1, *x_all, smem=1)
    egtot = totals_scan(gtot, -1)

    *both, gm, edge = timed(
        3.5, key_kernel, [((T, 2 * wide), f32)] * NY + [square, ((8, 128), f32)],
        parity, y1, uk, vb, gv_in, dq, dk, g_own, g_got, egtot, out, sel_k, smem=2,
        scratch=[states, pltpu.VMEM((TS, wide), f32)],
    )
    taps = conv_weight.shape[0]
    cw = jnp.transpose(conv_weight.reshape(taps, 2, NY, 64), (0, 2, 1, 3)).reshape(taps, 512)
    (gp,) = run(
        conv_back_kernel, [square], y1, gm, shift_open(edge, "z", -1), cw, smem=1,
        scratch=[pltpu.VMEM((TS + 8, 128), f32)],
    )
    blocks = [gp] + [shift(gp, "y", s) for s in (1, 2, 3)]
    keep, send, grad_own = timed(
        2.0, weight_kernel,
        [((NZ * T // 2, 512), f32), ((NZ * T // 2, 512), f32), ((T, 512), bf16)],
        jnp.stack([y, core]), *blocks, flipped, smem=1,
        scratch=[pltpu.VMEM((TS, 512), bf16)],
    )
    quarter = ((T, 512), f32)
    parts = run(
        split_x_kernel, [quarter] * NX, x.reshape(1), keep, swap(send, "core", 1), smem=1
    )
    own_rows = jnp.transpose(
        after(grad_own, parts[0]).reshape(T, NY, 2, 64), (0, 2, 1, 3)
    ).reshape(T, 512)
    grad_x = mm_nt(own_rows, qk_weight).astype(bf16)
    both = swap_y(lax.optimization_barrier((*both, keep))[:NY])
    mixed_out, grad_values = run(
        rows_kernel, [((T, H * V), bf16)] * 2, y1, *both, smem=1
    )
    parts = [parts[0]] + [shift(parts[s], "x", s) for s in (1, 2, 3)]
    parts[0] = after(parts[0], grad_x)
    for mask in (1, 2, 4):
        n = 64 // mask
        bit = lax.rem(lax.div(z, mask), 2).reshape(1)
        keep, send = run(
            split_z_kernel, [((n, 512), f32), ((n, 512), f32)], bit, *parts, smem=1
        )
        parts = [keep, swap(send, "z", mask)]
    parts[0] = after(parts[0], grad_values)
    (pair_rows,) = run(
        stack_kernel, [((32, 512), f32)], core.reshape(1), *parts,
        *[swap(a, "core", 1) for a in parts], smem=1,
    )
    stacks = [pair_rows] + [shift(pair_rows, "x", s) for s in (1, 2, 3)]
    (weight_grad,) = run(finish_kernel, [((T, 512), f32)], x.reshape(1), *stacks, smem=1)

    return (mixed_out[None], grad_x[None], grad_values[None], weight_grad)


def solution(mesh):
    inner = Mesh(mesh.devices.reshape(NX, NC, NZ, NY), ("x", "core", "z", "y"))
    rows = P(("x", "core"), ("z", "y"), None)
    return jax.shard_map(
        on_device,
        mesh=inner,
        in_specs=(rows, P(), P(), rows, rows),
        out_specs=(rows, rows, rows, P(("z", "y"), None)),
        check_vma=False,
    )
```

```python
import jax
import jax.numpy as jnp
import numpy as np
from jax import lax
from jax.experimental import pallas as pl
from jax.experimental.pallas import tpu as pltpu
from jax.sharding import Mesh, PartitionSpec as P

H = 16
F = 16
V = 128
NX, NC, NZ, NY = 4, 2, 8, 4
T = 128
TS = T * NY
HG = H // NY
E = 160
EP = 256
f32 = jnp.float32
bf16 = jnp.bfloat16


def feature_tables():
    first = np.zeros((128, 512), np.float32)
    weight = np.zeros((8, EP), np.float32)
    for f in range(128):
        i, d = f % 16, f // 16
        first[i, f] = 1
        first[(i + d) % 16, 128 + f] = 1
        weight[:, f] = 1 / 32 if d == 0 else 1 / 16
    for f in range(8):
        first[f, 256 + f] = 1
        first[f + 8, 384 + f] = 1
        weight[:, 128 + f] = 1 / 16
    for f in range(16):
        first[f, 256 + 8 + f] = 1
        first[16, 384 + 8 + f] = 0.5
        weight[:, 128 + 8 + f] = 1 / 4
    first[16, 256 + 24] = 0.5
    first[16, 384 + 24] = 0.5
    weight[:, 128 + 24] = 1
    sel_q = first.copy()
    sel_q[64:80] = first[:16]
    sel_k = first.copy()
    sel_k[32:48] = first[:16]
    return sel_q, sel_k, weight


SEL_Q, SEL_K, WEIGHT = feature_tables()
BIT_REVERSED = (0, 4, 2, 6, 1, 5, 3, 7)


def mm(a, b):
    return lax.dot_general(a, b, (((1,), (0,)), ((), ())), preferred_element_type=f32)


def mm_nt(a, b):
    return lax.dot_general(a, b, (((1,), (1,)), ((), ())), preferred_element_type=f32)


def mm_tn(a, b):
    return lax.dot_general(a, b, (((0,), (0,)), ((), ())), preferred_element_type=f32)


def run(kernel, outs, *args, scratch=(), smem=0, us=0.5, placed=(), far_outs=()):
    vm = pl.BlockSpec(memory_space=pltpu.VMEM)
    sm = pl.BlockSpec(memory_space=pltpu.SMEM)
    return pl.pallas_call(
        kernel,
        out_shape=[jax.ShapeDtypeStruct(s, d) for s, d in outs],
        in_specs=[
            sm if i < smem else pl.BlockSpec(memory_space=pltpu.HBM) if i in placed else vm
            for i in range(len(args))
        ],
        out_specs=[
            pl.BlockSpec(memory_space=pltpu.HBM) if i in far_outs else vm for i in range(len(outs))
        ],
        scratch_shapes=list(scratch),
        compiler_params=pltpu.CompilerParams(vmem_limit_bytes=12 << 20),
        cost_estimate=pl.CostEstimate(
            flops=0, bytes_accessed=int(us * 3.5e6), transcendentals=0
        ),
    )(*args)


def timed(us, *args, **kwargs):
    return run(*args, us=us, **kwargs)


def features(u, sel):
    x = mm(u, sel)
    return jnp.concatenate([x[:, :128] * x[:, 128:256], x[:, 256:384] * x[:, 384:]], 1)


def feature_grad(u, sel, grad):
    x = mm(u, sel)
    g1, g2 = grad[:, :128], grad[:, 128:]
    stacked = jnp.concatenate(
        [g1 * x[:, 128:256], g1 * x[:, :128], g2 * x[:, 384:], g2 * x[:, 256:384]], 1
    ).astype(bf16)
    return mm_nt(stacked, sel)


def causal(rows, r):
    row = lax.broadcasted_iota(jnp.int32, (T, rows), 0) + r * T
    col = lax.broadcasted_iota(jnp.int32, (T, rows), 1)
    return row >= col


def lanes(h):
    return pl.ds(pl.multiple_of(h * V, V), V)


def turned(y, s):
    return lax.rem(y[0] + (s + NY), NY)


def group_lanes(g, width):
    return pl.ds(pl.multiple_of(g * width, width), width)


def pack_kernel(y, a, *outs):
    for s, o in enumerate(outs):
        o[...] = a[:, group_lanes(turned(y, s), HG * V)].astype(f32)


def fetch(blocks, buffer, sems):
    copies = [pltpu.make_async_copy(b, buffer.at[s], sems.at[s]) for s, b in enumerate(blocks)]
    for c in copies:
        c.start()
    return copies


def after(value, *others):
    return lax.optimization_barrier((value, *others))[0]


def pack_columns_kernel(y, a, *outs):
    for s, o in enumerate(outs):
        for k in range(NZ):
            o[:, k * T : (k + 1) * T] = a[:, group_lanes(turned(y, s) + k * NY, T)].astype(f32)


def flip_kernel(y, a0, a1, a2, a3, flipped):
    for s, a in enumerate((a0, a1, a2, a3)):
        cols = group_lanes(turned(y, -s), T)
        for k in range(NZ):
            t = jnp.transpose(a[:, k * T : (k + 1) * T]).astype(bf16)
            for part in range(NC * NX):
                at = part * T + BIT_REVERSED[k] * 16
                flipped[at : at + 16, cols] = t[part * 16 : part * 16 + 16]


def mix_kernel(y, projected, halo, cw, o0, o1, o2, o3, pad, blocks):
    pad[:8] = halo[...]
    pad[8:] = projected[...]
    m = projected[...] * cw[0:1]
    for j in (1, 2):
        m += pad[8 - j : 8 - j + T] * cw[j : j + 1]
    lane = lax.broadcasted_iota(jnp.int32, (T, 128), 1)
    for g in range(NY):
        at = (g // 2) * 128
        q, k = m[:, at : at + 128], m[:, 256 + at : 256 + at + 128]
        if g % 2:
            q = pltpu.roll(q, 64, 1)
        else:
            k = pltpu.roll(k, 64, 1)
        blocks[g] = jnp.where(lane < 64, q, k)
    for s, o in enumerate((o0, o1, o2, o3)):
        o[...] = blocks[turned(y, s)]


def prepare_kernel(y, b0, b1, b2, b3, sel_k, w, uq, uk, tot, mg):
    for s, b in enumerate((b0, b1, b2, b3)):
        mg[group_lanes(turned(y, -s), T)] = b[...]
    lane = lax.broadcasted_iota(jnp.int32, (TS, 128), 1)
    tot[...] = jnp.zeros_like(tot)

    def one(h, _):
        for is_key in (0, 1):
            x = pltpu.roll(mg[...], (256 - 64 * is_key) - 16 * h, 1)
            hi = x.astype(bf16).astype(f32)
            lo = x - hi
            a, b = (lo, hi) if is_key else (hi, lo)
            u = jnp.where(lane < 16, hi, jnp.where(lane == 16, 2.0, 0.0))
            u = jnp.where((lane >= 32) & (lane < 48), pltpu.roll(a, 32, 1), u)
            u = jnp.where((lane >= 64) & (lane < 80), pltpu.roll(b, 64, 1), u)
            (uk if is_key else uq)[h] = u.astype(bf16)
        rk = features(uk[h], sel_k[...])
        tot[pl.ds(h, 1)] = jnp.sum(rk, 0, keepdims=True) * w[0:1]
        return 0

    lax.fori_loop(0, HG, one, 0)


def halves(scratch, p, keep, send):
    keep[...] = scratch[p]
    send[...] = scratch[1 - p]


def state_kernel(
    p, y, uq, uk, v0, v1, v2, v3, sel_k, w, keep, send, vb, rs, scratch, buffer, sems
):
    copies = fetch((v0, v1, v2, v3), buffer, sems)
    for s in range(NY):
        copies[s].wait()
        vb[group_lanes(turned(y, -s), T)] = buffer[s].astype(bf16)

    def one(h, _):
        rk = (features(uk[h], sel_k[...]) * w[0:1]).astype(bf16)
        s = mm_tn(rk, vb[:, lanes(h)])
        scratch[lax.div(h, 2), pl.ds(pl.multiple_of(lax.rem(h, 2) * E, E), E)] = s[:E]
        for r in range(NY):
            rows = (r + 1) * T
            t = mm_nt(uq[h, r * T : rows], uk[h, :rows])
            t = jnp.where(causal(rows, r), 0.5 + t * t * (1 / 32), 0.0)
            rs[h, r * T : rows] = jnp.broadcast_to(jnp.sum(t, 1, keepdims=True), (T, V))
        return 0

    lax.fori_loop(0, HG, one, 0)
    halves(scratch, p[0], keep, send)


def denom_kernel(
    p, y, uq, rs, etot, c0, c1, c2, c3, sel_q, w, keep, send, dn, inv, scratch, buffer, sems
):
    for c in fetch((c0, c1, c2, c3), buffer, sems):
        c.wait()
    def one(h, _):
        rq = features(uq[h], sel_q[...])
        den = rs[h] + jnp.sum(rq * etot[pl.ds(h, 1)], 1, keepdims=True)
        iv = 1.0 / den
        inv[h] = iv
        for s in range(NY):
            rows = group_lanes(turned(y, -s), T)
            dn[rows, lanes(h)] = (buffer[s, :, lanes(h)] * inv[h, rows]).astype(bf16)
        s = mm_tn((rq * w[0:1]).astype(bf16), dn[:, lanes(h)])
        scratch[lax.div(h, 2), pl.ds(pl.multiple_of(lax.rem(h, 2) * E, E), E)] = s[:E]
        return 0

    lax.fori_loop(0, HG, one, 0)
    halves(scratch, p[0], keep, send)


def pair_kernel(use, keep, got, e0, e1, e2, own, partner):
    base = e0[...] + e1[...] + e2[...]
    own[...] = base + jnp.where(use[0] > 0, got[...], 0.0)
    partner[...] = base + jnp.where(use[0] > 0, 0.0, keep[...])


def fill_states(p, own, got, scratch):
    zero = jnp.zeros((EP - E, V), bf16)
    for which, a in ((p, own), (1 - p, got)):
        for i in range(2):
            scratch[2 * which + i, :E] = a[i * E : (i + 1) * E].astype(bf16)
            scratch[2 * which + i, E:] = zero


def local_kernel(
    p, uq, uk, vb, dn, inv, etot, own, got, sel_q, w, out, dq, gv, dk, gtot, dk_acc, states
):
    lane = lax.broadcasted_iota(jnp.int32, (TS, 128), 1)
    gtot[...] = jnp.zeros_like(gtot)
    dq[...] = jnp.zeros_like(dq)
    dk[...] = jnp.zeros_like(dk)
    fill_states(p[0], own, got, states)

    def one(h, _):
        cols = lanes(h)
        c = states[h]
        tot_row = etot[pl.ds(h, 1)]
        gsum = jnp.zeros((1, EP), f32)
        grads = []
        for r in reversed(range(NY)):
            rows = (r + 1) * T
            mine = slice(r * T, rows)
            u = uq[h, mine]
            keep = causal(rows, r)
            s = mm_nt(u, uk[h, :rows])
            pr = jnp.where(keep, 0.5 + s * s * (1 / 32), 0.0).astype(bf16)
            rq = features(u, sel_q[...])
            numer = mm(pr, vb[:rows, cols]) + mm(rq.astype(bf16), c)
            o = numer * inv[h, mine]
            out[r, :, cols] = o
            d = dn[mine, cols]
            dd = -jnp.sum(d.astype(f32) * o, 1, keepdims=True)
            dp = mm_nt(d, vb[:rows, cols]) + dd
            ds = jnp.where(keep, dp * s * (1 / 16), 0.0).astype(bf16)
            gsum += jnp.sum(rq * dd, 0, keepdims=True)
            dr = mm_nt(d, c) + dd * tot_row
            grads.append(mm(ds, uk[h, :rows]) + feature_grad(u, sel_q[...], dr))
            gv_add = mm_tn(pr, d)
            dk_add = mm_tn(ds, u)
            if r == NY - 1:
                gv[:, cols] = gv_add
                dk_acc[...] = dk_add
            else:
                gv[:rows, cols] += gv_add
                dk_acc[:rows] += dk_add
        gtot[pl.ds(h, 1)] = gsum * w[0:1]
        g = jnp.concatenate(grads[::-1], 0)
        dq[...] += pltpu.roll(jnp.where(lane < 16, g, 0.0), 16 * h, 1)
        dk[...] += pltpu.roll(jnp.where(lane < 16, dk_acc[...], 0.0), 64 + 16 * h, 1)
        return 0

    lax.fori_loop(0, HG, one, 0)


def key_kernel(
    p, y, uk, vb, gv_in, dq, dk, own, got, egtot, out, sel_k,
    o0, o1, o2, o3, gm, edge, states, gv, sems,
):
    lane = lax.broadcasted_iota(jnp.int32, (TS, 128), 1)
    copies = [
        pltpu.make_async_copy(out.at[turned(y, s)], o.at[:, pl.ds(0, HG * V)], sems.at[s])
        for s, o in enumerate((o0, o1, o2, o3))
    ]
    for c in copies:
        c.start()
    fill_states(p[0], own, got, states)
    gm[...] = dq[...] + dk[...]

    def one(h, _):
        cols = lanes(h)
        c = states[h]
        rk = features(uk[h], sel_k[...]).astype(bf16)
        gv[:, cols] = gv_in[:, cols] + mm(rk, c)
        dr = mm_nt(vb[:, cols], c) + egtot[pl.ds(h, 1)]
        g = feature_grad(uk[h], sel_k[...], dr)
        gm[...] += pltpu.roll(jnp.where(lane < 16, g, 0.0), 64 + 16 * h, 1)
        return 0

    lax.fori_loop(0, HG, one, 0)
    edge[...] = gm[:8]
    for s, o in enumerate((o0, o1, o2, o3)):
        copies.append(
            pltpu.make_async_copy(
                gv.at[group_lanes(turned(y, s), T)], o.at[:, pl.ds(HG * V, HG * V)], sems.at[NY + s]
            )
        )
        copies[-1].start()
    for c in copies:
        c.wait()


def conv_back_kernel(y, gm, halo, cw, gp, pad):
    pad[:TS] = gm[...]
    pad[TS:] = halo[...]
    cols = group_lanes(y[0], 128)
    total = gm[...] * cw[0:1, cols]
    for j in (1, 2):
        total += pad[j : TS + j] * cw[j : j + 1, cols]
    gp[...] = total


def weight_kernel(at, g0, g1, g2, g3, flipped, keep, send, grad_own, gp):
    y, core = at[0], at[1]
    for s, g in enumerate((g0, g1, g2, g3)):
        gp[:, group_lanes(turned(at, -s), 128)] = g[...].astype(bf16)
    half = NZ * T // 2
    for which, ref in ((1 - core, send), (core, keep)):
        ref[...] = mm(flipped[group_lanes(which, half)], gp[...])
    grad_own[...] = gp[group_lanes(y, T)]


def split_x_kernel(x, a, b, o0, o1, o2, o3):
    for s, o in enumerate((o0, o1, o2, o3)):
        rows = pl.ds(pl.multiple_of(lax.rem(x[0] + s, NX) * T, T), T)
        o[...] = a[rows] + b[rows]


def split_z_kernel(bit, *refs):
    ins, (keep, send) = refs[:-2], refs[-2:]
    n = keep.shape[0]
    for which, o in ((bit[0], keep), (1 - bit[0], send)):
        rows = pl.ds(pl.multiple_of(which * n, n), n)
        total = ins[0][rows]
        for a in ins[1:]:
            total += a[rows]
        o[...] = total


def stack_kernel(core, a, b, c, d, o):
    total = a[...] + b[...]
    o[group_lanes(core[0], 16)] = total
    o[group_lanes(1 - core[0], 16)] = c[...] + d[...]


def finish_kernel(x, m0, m1, m2, m3, rows):
    lane = lax.broadcasted_iota(jnp.int32, (16, 128), 1)
    for s, m in enumerate((m0, m1, m2, m3)):
        src = lax.rem(x[0] - s + NX, NX)
        for core in range(NC):
            at = pl.ds(pl.multiple_of(core * 64 + src * 16, 16), 16)
            b = m[core * 16 : core * 16 + 16]
            for half in range(2):
                lo, hi = b[:, half * 256 : half * 256 + 128], b[:, half * 256 + 128 : half * 256 + 256]
                q = jnp.where(lane < 64, lo, pltpu.roll(hi, 64, 1))
                k = jnp.where(lane < 64, pltpu.roll(lo, 64, 1), hi)
                rows[at, half * 128 : half * 128 + 128] = q
                rows[at, 256 + half * 128 : 256 + half * 128 + 128] = k


def rows_kernel(y, b0, b1, b2, b3, out, grad):
    for s, b in enumerate((b0, b1, b2, b3)):
        cols = group_lanes(turned(y, -s), HG * V)
        out[:, cols] = b[:, : HG * V].astype(bf16)
        grad[:, cols] = b[:, HG * V :].astype(bf16)


def shift(value, axis, by):
    n = lax.axis_size(axis)
    return lax.ppermute(value, axis, [(i, (i + by) % n) for i in range(n)])


def shift_open(value, axis, by):
    n = lax.axis_size(axis)
    return lax.ppermute(
        value, axis, [(i, i + by) for i in range(n) if 0 <= i + by < n]
    )


def swap(value, axis, mask):
    n = lax.axis_size(axis)
    return lax.ppermute(value, axis, [(i, i ^ mask) for i in range(n)])


def totals_scan(tot, sign):
    before = shift_open(tot, "z", sign)
    before = before + shift_open(before + tot, "z", 2 * sign)
    return before + shift_open(before + tot, "z", 4 * sign)


def across_pairs(keep, got, sign):
    total = keep + got
    return [shift_open(total, "z", sign * d) for d in (2, 4, 6)]


def back_to_pair(keep, got, others, use):
    half = ((2 * E, V), f32)
    own, partner = run(pair_kernel, [half, half], use, keep, got, *others, smem=1)
    return own, swap(partner, "z", 1)


def swap_y(blocks):
    return [blocks[0]] + [shift(blocks[s], "y", s) for s in (1, 2, 3)]


def on_device(tokens, qk_weight, conv_weight, values, cotangent):
    def place(name):
        return lax.axis_index(name).astype(jnp.int32)

    x, core, z, y = place("x"), place("core"), place("z"), place("y")
    y1, parity = y.reshape(1), lax.rem(z, 2).reshape(1)
    sel_q, sel_k = jnp.asarray(SEL_Q, bf16), jnp.asarray(SEL_K, bf16)
    w = jnp.asarray(WEIGHT, f32)
    local_x = tokens[0]
    wide = HG * V

    by_head = [((T, wide), f32)] * NY
    v_all = swap_y(run(pack_kernel, by_head, y1, values[0], smem=1))
    projected = jnp.dot(local_x, qk_weight, preferred_element_type=f32)
    halo = lax.ppermute(
        projected[T - 8 :], ("z", "y"), [(i, i + 1) for i in range(NZ * NY - 1)]
    )
    mixed = run(
        mix_kernel, [((T, 128), f32)] * NY, y1, after(projected, *v_all[1:]), halo, conv_weight, smem=1,
        scratch=[pltpu.VMEM((T + 8, 512), f32), pltpu.VMEM((NY, T, 128), f32)],
    )
    mixed = swap_y(mixed)
    uq, uk, tot = timed(
        2.6, prepare_kernel,
        [((HG, TS, 128), bf16), ((HG, TS, 128), bf16), ((8, EP), f32)],
        y1, *mixed, sel_k, w, smem=1, scratch=[pltpu.VMEM((TS, 128), f32)],
    )
    c_all = swap_y(run(pack_kernel, by_head, y1, after(cotangent[0], tot), smem=1))
    etot = totals_scan(tot, 1)
    half = ((2 * E, V), f32)
    half_scratch = [
        pltpu.VMEM((2, 2 * E, V), f32), pltpu.VMEM((NY, T, wide), f32),
        pltpu.SemaphoreType.DMA((NY,)),
    ]
    keep, send, vb, rs = timed(
        2.8, state_kernel, [half, half, ((TS, wide), bf16), ((HG, TS, V), f32)],
        parity, y1, uq, uk, *v_all, sel_k, w, smem=2, scratch=half_scratch,
        placed=(4, 5, 6, 7),
    )
    g_keep, g_send, dn, inv = timed(
        2.4, denom_kernel, [half, half, ((TS, wide), bf16), ((HG, TS, V), f32)],
        parity, y1, uq, rs, etot, *c_all, sel_q, w, smem=2, scratch=half_scratch,
        placed=(5, 6, 7, 8),
    )
    pair = swap(after(send, etot), "z", 1)
    g_pair = swap(g_send, "z", 1)
    earlier = across_pairs(keep, pair, 1)
    g_later = across_pairs(g_keep, g_pair, -1)
    own, got = back_to_pair(keep, after(pair, g_pair), earlier, parity)
    g_own, g_got = back_to_pair(g_keep, g_pair, g_later, 1 - parity)
    own = after(own, g_own)

    states = pltpu.VMEM((HG, EP, V), bf16)
    square = ((TS, 128), f32)
    out, dq, gv_in, dk, gtot = timed(
        9.5, local_kernel,
        [((NY, T, wide), f32), square, ((TS, wide), f32), square, ((8, EP), f32)],
        parity, uq, uk, vb, dn, inv, etot, own, got, sel_q, w, smem=1,
        scratch=[pltpu.VMEM((TS, 128), f32), states],
    )
    x_packed = timed(
        1.5, pack_columns_kernel, [((T, NZ * T), f32)] * NY, y1, after(local_x, etot), smem=1
    )
    x_all = swap_y(lax.optimization_barrier((*x_packed, g_keep))[:NY])
    (flipped,) = timed(1.9, flip_kernel, [((NZ * T, TS), bf16)], y1, *x_all, smem=1)
    egtot = totals_scan(gtot, -1)

    *both, gm, edge = timed(
        3.5, key_kernel, [((T, 2 * wide), f32)] * NY + [square, ((8, 128), f32)],
        parity, y1, uk, vb, gv_in, dq, dk, g_own, g_got, egtot, out, sel_k, smem=2,
        scratch=[states, pltpu.VMEM((TS, wide), f32), pltpu.SemaphoreType.DMA((2 * NY,))],
        far_outs=(0, 1, 2, 3),
    )
    taps = conv_weight.shape[0]
    cw = jnp.transpose(conv_weight.reshape(taps, 2, NY, 64), (0, 2, 1, 3)).reshape(taps, 512)
    (gp,) = run(
        conv_back_kernel, [square], y1, gm, shift_open(edge, "z", -1), cw, smem=1,
        scratch=[pltpu.VMEM((TS + 8, 128), f32)],
    )
    blocks = [gp] + [shift(gp, "y", s) for s in (1, 2, 3)]
    keep, send, grad_own = timed(
        2.0, weight_kernel,
        [((NZ * T // 2, 512), f32), ((NZ * T // 2, 512), f32), ((T, 512), bf16)],
        jnp.stack([y, core]), *blocks, flipped, smem=1,
        scratch=[pltpu.VMEM((TS, 512), bf16)],
    )
    quarter = ((T, 512), f32)
    parts = run(
        split_x_kernel, [quarter] * NX, x.reshape(1), keep, swap(send, "core", 1), smem=1
    )
    own_rows = jnp.transpose(
        after(grad_own, parts[0]).reshape(T, NY, 2, 64), (0, 2, 1, 3)
    ).reshape(T, 512)
    grad_x = mm_nt(own_rows, qk_weight).astype(bf16)
    parts = [parts[0]] + [shift(parts[s], "x", s) for s in (1, 2, 3)]
    parts[0] = after(parts[0], grad_x)
    both = swap_y(lax.optimization_barrier((*both, parts[1]))[:NY])
    mixed_out, grad_values = run(
        rows_kernel, [((T, H * V), bf16)] * 2, y1, *both, smem=1
    )
    for mask in (1, 2, 4):
        n = 64 // mask
        bit = lax.rem(lax.div(z, mask), 2).reshape(1)
        keep, send = run(
            split_z_kernel, [((n, 512), f32), ((n, 512), f32)], bit, *parts, smem=1
        )
        parts = [keep, swap(send, "z", mask)]
    (pair_rows,) = run(
        stack_kernel, [((32, 512), f32)], core.reshape(1), *parts,
        *[swap(a, "core", 1) for a in parts], smem=1,
    )
    stacks = [pair_rows] + [shift(pair_rows, "x", s) for s in (1, 2, 3)]
    stacks[0] = after(stacks[0], grad_values)
    (weight_grad,) = run(finish_kernel, [((T, 512), f32)], x.reshape(1), *stacks, smem=1)

    return (mixed_out[None], grad_x[None], grad_values[None], weight_grad)


def solution(mesh):
    inner = Mesh(mesh.devices.reshape(NX, NC, NZ, NY), ("x", "core", "z", "y"))
    rows = P(("x", "core"), ("z", "y"), None)
    return jax.shard_map(
        on_device,
        mesh=inner,
        in_specs=(rows, P(), P(), rows, rows),
        out_specs=(rows, rows, rows, P(("z", "y"), None)),
        check_vma=False,
    )
```

```python
import jax
import jax.numpy as jnp
import numpy as np
from jax import lax
from jax.experimental import pallas as pl
from jax.experimental.pallas import tpu as pltpu
from jax.sharding import Mesh, PartitionSpec as P

H = 16
F = 16
V = 128
NX, NC, NZ, NY = 4, 2, 8, 4
T = 128
TS = T * NY
HG = H // NY
E = 160
EP = 256
f32 = jnp.float32
bf16 = jnp.bfloat16


def feature_tables():
    first = np.zeros((128, 512), np.float32)
    weight = np.zeros((8, EP), np.float32)
    for f in range(128):
        i, d = f % 16, f // 16
        first[i, f] = 1
        first[(i + d) % 16, 128 + f] = 1
        weight[:, f] = 1 / 32 if d == 0 else 1 / 16
    for f in range(8):
        first[f, 256 + f] = 1
        first[f + 8, 384 + f] = 1
        weight[:, 128 + f] = 1 / 16
    for f in range(16):
        first[f, 256 + 8 + f] = 1
        first[16, 384 + 8 + f] = 0.5
        weight[:, 128 + 8 + f] = 1 / 4
    first[16, 256 + 24] = 0.5
    first[16, 384 + 24] = 0.5
    weight[:, 128 + 24] = 1
    sel_q = first.copy()
    sel_q[64:80] = first[:16]
    sel_k = first.copy()
    sel_k[32:48] = first[:16]
    return sel_q, sel_k, weight


SEL_Q, SEL_K, WEIGHT = feature_tables()
BIT_REVERSED = (0, 4, 2, 6, 1, 5, 3, 7)


def mm(a, b):
    return lax.dot_general(a, b, (((1,), (0,)), ((), ())), preferred_element_type=f32)


def mm_nt(a, b):
    return lax.dot_general(a, b, (((1,), (1,)), ((), ())), preferred_element_type=f32)


def mm_tn(a, b):
    return lax.dot_general(a, b, (((0,), (0,)), ((), ())), preferred_element_type=f32)


def run(kernel, outs, *args, scratch=(), smem=0, us=0.5, placed=(), far_outs=()):
    vm = pl.BlockSpec(memory_space=pltpu.VMEM)
    sm = pl.BlockSpec(memory_space=pltpu.SMEM)
    return pl.pallas_call(
        kernel,
        out_shape=[
            pltpu.HBM(s, d) if i in far_outs else jax.ShapeDtypeStruct(s, d)
            for i, (s, d) in enumerate(outs)
        ],
        in_specs=[
            sm if i < smem else pl.BlockSpec(memory_space=pltpu.HBM) if i in placed else vm
            for i in range(len(args))
        ],
        out_specs=[
            pl.BlockSpec(memory_space=pltpu.HBM) if i in far_outs else vm for i in range(len(outs))
        ],
        scratch_shapes=list(scratch),
        compiler_params=pltpu.CompilerParams(vmem_limit_bytes=12 << 20),
        cost_estimate=pl.CostEstimate(
            flops=0, bytes_accessed=int(us * 3.5e6), transcendentals=0
        ),
    )(
        *[
            pltpu.with_memory_space_constraint(a, pltpu.HBM) if i in placed else a
            for i, a in enumerate(args)
        ]
    )


def timed(us, *args, **kwargs):
    return run(*args, us=us, **kwargs)


def features(u, sel):
    x = mm(u, sel)
    return jnp.concatenate([x[:, :128] * x[:, 128:256], x[:, 256:384] * x[:, 384:]], 1)


def feature_grad(u, sel, grad):
    x = mm(u, sel)
    g1, g2 = grad[:, :128], grad[:, 128:]
    stacked = jnp.concatenate(
        [g1 * x[:, 128:256], g1 * x[:, :128], g2 * x[:, 384:], g2 * x[:, 256:384]], 1
    ).astype(bf16)
    return mm_nt(stacked, sel)


def causal(rows, r):
    row = lax.broadcasted_iota(jnp.int32, (T, rows), 0) + r * T
    col = lax.broadcasted_iota(jnp.int32, (T, rows), 1)
    return row >= col


def lanes(h):
    return pl.ds(pl.multiple_of(h * V, V), V)


def turned(y, s):
    return lax.rem(y[0] + (s + NY), NY)


def group_lanes(g, width):
    return pl.ds(pl.multiple_of(g * width, width), width)


def pack_kernel(y, a, *outs):
    for s, o in enumerate(outs):
        o[...] = a[:, group_lanes(turned(y, s), HG * V)].astype(f32)


def fetch(blocks, buffer, sems):
    copies = [pltpu.make_async_copy(b, buffer.at[s], sems.at[s]) for s, b in enumerate(blocks)]
    for c in copies:
        c.start()
    return copies


def after(value, *others):
    return lax.optimization_barrier((value, *others))[0]


def pack_columns_kernel(y, a, *outs):
    for s, o in enumerate(outs):
        for k in range(NZ):
            o[:, k * T : (k + 1) * T] = a[:, group_lanes(turned(y, s) + k * NY, T)].astype(f32)


def flip_kernel(y, a0, a1, a2, a3, flipped):
    for s, a in enumerate((a0, a1, a2, a3)):
        cols = group_lanes(turned(y, -s), T)
        for k in range(NZ):
            t = jnp.transpose(a[:, k * T : (k + 1) * T]).astype(bf16)
            for part in range(NC * NX):
                at = part * T + BIT_REVERSED[k] * 16
                flipped[at : at + 16, cols] = t[part * 16 : part * 16 + 16]


def mix_kernel(y, projected, halo, cw, o0, o1, o2, o3, pad, blocks):
    pad[:8] = halo[...]
    pad[8:] = projected[...]
    m = projected[...] * cw[0:1]
    for j in (1, 2):
        m += pad[8 - j : 8 - j + T] * cw[j : j + 1]
    lane = lax.broadcasted_iota(jnp.int32, (T, 128), 1)
    for g in range(NY):
        at = (g // 2) * 128
        q, k = m[:, at : at + 128], m[:, 256 + at : 256 + at + 128]
        if g % 2:
            q = pltpu.roll(q, 64, 1)
        else:
            k = pltpu.roll(k, 64, 1)
        blocks[g] = jnp.where(lane < 64, q, k)
    for s, o in enumerate((o0, o1, o2, o3)):
        o[...] = blocks[turned(y, s)]


def prepare_kernel(y, b0, b1, b2, b3, sel_k, w, uq, uk, tot, mg):
    for s, b in enumerate((b0, b1, b2, b3)):
        mg[group_lanes(turned(y, -s), T)] = b[...]
    lane = lax.broadcasted_iota(jnp.int32, (TS, 128), 1)
    tot[...] = jnp.zeros_like(tot)

    def one(h, _):
        for is_key in (0, 1):
            x = pltpu.roll(mg[...], (256 - 64 * is_key) - 16 * h, 1)
            hi = x.astype(bf16).astype(f32)
            lo = x - hi
            a, b = (lo, hi) if is_key else (hi, lo)
            u = jnp.where(lane < 16, hi, jnp.where(lane == 16, 2.0, 0.0))
            u = jnp.where((lane >= 32) & (lane < 48), pltpu.roll(a, 32, 1), u)
            u = jnp.where((lane >= 64) & (lane < 80), pltpu.roll(b, 64, 1), u)
            (uk if is_key else uq)[h] = u.astype(bf16)
        rk = features(uk[h], sel_k[...])
        tot[pl.ds(h, 1)] = jnp.sum(rk, 0, keepdims=True) * w[0:1]
        return 0

    lax.fori_loop(0, HG, one, 0)


def halves(scratch, p, keep, send):
    keep[...] = scratch[p]
    send[...] = scratch[1 - p]


def state_kernel(
    p, y, uq, uk, v0, v1, v2, v3, sel_k, w, keep, send, vb, rs, scratch, buffer, sems
):
    copies = fetch((v0, v1, v2, v3), buffer, sems)
    for s in range(NY):
        copies[s].wait()
        vb[group_lanes(turned(y, -s), T)] = buffer[s].astype(bf16)

    def one(h, _):
        rk = (features(uk[h], sel_k[...]) * w[0:1]).astype(bf16)
        s = mm_tn(rk, vb[:, lanes(h)])
        scratch[lax.div(h, 2), pl.ds(pl.multiple_of(lax.rem(h, 2) * E, E), E)] = s[:E]
        for r in range(NY):
            rows = (r + 1) * T
            t = mm_nt(uq[h, r * T : rows], uk[h, :rows])
            t = jnp.where(causal(rows, r), 0.5 + t * t * (1 / 32), 0.0)
            rs[h, r * T : rows] = jnp.broadcast_to(jnp.sum(t, 1, keepdims=True), (T, V))
        return 0

    lax.fori_loop(0, HG, one, 0)
    halves(scratch, p[0], keep, send)


def denom_kernel(
    p, y, uq, rs, etot, c0, c1, c2, c3, sel_q, w, keep, send, dn, inv, scratch, buffer, sems
):
    for c in fetch((c0, c1, c2, c3), buffer, sems):
        c.wait()
    def one(h, _):
        rq = features(uq[h], sel_q[...])
        den = rs[h] + jnp.sum(rq * etot[pl.ds(h, 1)], 1, keepdims=True)
        iv = 1.0 / den
        inv[h] = iv
        for s in range(NY):
            rows = group_lanes(turned(y, -s), T)
            dn[rows, lanes(h)] = (buffer[s, :, lanes(h)] * inv[h, rows]).astype(bf16)
        s = mm_tn((rq * w[0:1]).astype(bf16), dn[:, lanes(h)])
        scratch[lax.div(h, 2), pl.ds(pl.multiple_of(lax.rem(h, 2) * E, E), E)] = s[:E]
        return 0

    lax.fori_loop(0, HG, one, 0)
    halves(scratch, p[0], keep, send)


def pair_kernel(use, keep, got, e0, e1, e2, own, partner):
    base = e0[...] + e1[...] + e2[...]
    own[...] = base + jnp.where(use[0] > 0, got[...], 0.0)
    partner[...] = base + jnp.where(use[0] > 0, 0.0, keep[...])


def fill_states(p, own, got, scratch):
    zero = jnp.zeros((EP - E, V), bf16)
    for which, a in ((p, own), (1 - p, got)):
        for i in range(2):
            scratch[2 * which + i, :E] = a[i * E : (i + 1) * E].astype(bf16)
            scratch[2 * which + i, E:] = zero


def local_kernel(
    p, uq, uk, vb, dn, inv, etot, own, got, sel_q, w, out, dq, gv, dk, gtot, dk_acc, states
):
    lane = lax.broadcasted_iota(jnp.int32, (TS, 128), 1)
    gtot[...] = jnp.zeros_like(gtot)
    dq[...] = jnp.zeros_like(dq)
    dk[...] = jnp.zeros_like(dk)
    fill_states(p[0], own, got, states)

    def one(h, _):
        cols = lanes(h)
        c = states[h]
        tot_row = etot[pl.ds(h, 1)]
        gsum = jnp.zeros((1, EP), f32)
        grads = []
        for r in reversed(range(NY)):
            rows = (r + 1) * T
            mine = slice(r * T, rows)
            u = uq[h, mine]
            keep = causal(rows, r)
            s = mm_nt(u, uk[h, :rows])
            pr = jnp.where(keep, 0.5 + s * s * (1 / 32), 0.0).astype(bf16)
            rq = features(u, sel_q[...])
            numer = mm(pr, vb[:rows, cols]) + mm(rq.astype(bf16), c)
            o = numer * inv[h, mine]
            out[r, :, cols] = o
            d = dn[mine, cols]
            dd = -jnp.sum(d.astype(f32) * o, 1, keepdims=True)
            dp = mm_nt(d, vb[:rows, cols]) + dd
            ds = jnp.where(keep, dp * s * (1 / 16), 0.0).astype(bf16)
            gsum += jnp.sum(rq * dd, 0, keepdims=True)
            dr = mm_nt(d, c) + dd * tot_row
            grads.append(mm(ds, uk[h, :rows]) + feature_grad(u, sel_q[...], dr))
            gv_add = mm_tn(pr, d)
            dk_add = mm_tn(ds, u)
            if r == NY - 1:
                gv[:, cols] = gv_add
                dk_acc[...] = dk_add
            else:
                gv[:rows, cols] += gv_add
                dk_acc[:rows] += dk_add
        gtot[pl.ds(h, 1)] = gsum * w[0:1]
        g = jnp.concatenate(grads[::-1], 0)
        dq[...] += pltpu.roll(jnp.where(lane < 16, g, 0.0), 16 * h, 1)
        dk[...] += pltpu.roll(jnp.where(lane < 16, dk_acc[...], 0.0), 64 + 16 * h, 1)
        return 0

    lax.fori_loop(0, HG, one, 0)


def key_kernel(
    p, y, uk, vb, gv_in, dq, dk, own, got, egtot, out, sel_k,
    o0, o1, o2, o3, gm, edge, states, gv, sems,
):
    lane = lax.broadcasted_iota(jnp.int32, (TS, 128), 1)
    copies = [
        pltpu.make_async_copy(out.at[turned(y, s)], o.at[:, pl.ds(0, HG * V)], sems.at[s])
        for s, o in enumerate((o0, o1, o2, o3))
    ]
    for c in copies:
        c.start()
    fill_states(p[0], own, got, states)
    gm[...] = dq[...] + dk[...]

    def one(h, _):
        cols = lanes(h)
        c = states[h]
        rk = features(uk[h], sel_k[...]).astype(bf16)
        gv[:, cols] = gv_in[:, cols] + mm(rk, c)
        dr = mm_nt(vb[:, cols], c) + egtot[pl.ds(h, 1)]
        g = feature_grad(uk[h], sel_k[...], dr)
        gm[...] += pltpu.roll(jnp.where(lane < 16, g, 0.0), 64 + 16 * h, 1)
        return 0

    lax.fori_loop(0, HG, one, 0)
    edge[...] = gm[:8]
    for s, o in enumerate((o0, o1, o2, o3)):
        copies.append(
            pltpu.make_async_copy(
                gv.at[group_lanes(turned(y, s), T)], o.at[:, pl.ds(HG * V, HG * V)], sems.at[NY + s]
            )
        )
        copies[-1].start()
    for c in copies:
        c.wait()


def conv_back_kernel(y, gm, halo, cw, gp, pad):
    pad[:TS] = gm[...]
    pad[TS:] = halo[...]
    cols = group_lanes(y[0], 128)
    total = gm[...] * cw[0:1, cols]
    for j in (1, 2):
        total += pad[j : TS + j] * cw[j : j + 1, cols]
    gp[...] = total


def weight_kernel(at, g0, g1, g2, g3, flipped, keep, send, grad_own, gp):
    y, core = at[0], at[1]
    for s, g in enumerate((g0, g1, g2, g3)):
        gp[:, group_lanes(turned(at, -s), 128)] = g[...].astype(bf16)
    half = NZ * T // 2
    for which, ref in ((1 - core, send), (core, keep)):
        ref[...] = mm(flipped[group_lanes(which, half)], gp[...])
    grad_own[...] = gp[group_lanes(y, T)]


def split_x_kernel(x, a, b, o0, o1, o2, o3):
    for s, o in enumerate((o0, o1, o2, o3)):
        rows = pl.ds(pl.multiple_of(lax.rem(x[0] + s, NX) * T, T), T)
        o[...] = a[rows] + b[rows]


def split_z_kernel(bit, *refs):
    ins, (keep, send) = refs[:-2], refs[-2:]
    n = keep.shape[0]
    for which, o in ((bit[0], keep), (1 - bit[0], send)):
        rows = pl.ds(pl.multiple_of(which * n, n), n)
        total = ins[0][rows]
        for a in ins[1:]:
            total += a[rows]
        o[...] = total


def stack_kernel(core, a, b, c, d, o):
    total = a[...] + b[...]
    o[group_lanes(core[0], 16)] = total
    o[group_lanes(1 - core[0], 16)] = c[...] + d[...]


def finish_kernel(x, m0, m1, m2, m3, rows):
    lane = lax.broadcasted_iota(jnp.int32, (16, 128), 1)
    for s, m in enumerate((m0, m1, m2, m3)):
        src = lax.rem(x[0] - s + NX, NX)
        for core in range(NC):
            at = pl.ds(pl.multiple_of(core * 64 + src * 16, 16), 16)
            b = m[core * 16 : core * 16 + 16]
            for half in range(2):
                lo, hi = b[:, half * 256 : half * 256 + 128], b[:, half * 256 + 128 : half * 256 + 256]
                q = jnp.where(lane < 64, lo, pltpu.roll(hi, 64, 1))
                k = jnp.where(lane < 64, pltpu.roll(lo, 64, 1), hi)
                rows[at, half * 128 : half * 128 + 128] = q
                rows[at, 256 + half * 128 : 256 + half * 128 + 128] = k


def rows_kernel(y, b0, b1, b2, b3, out, grad):
    for s, b in enumerate((b0, b1, b2, b3)):
        cols = group_lanes(turned(y, -s), HG * V)
        out[:, cols] = b[:, : HG * V].astype(bf16)
        grad[:, cols] = b[:, HG * V :].astype(bf16)


def shift(value, axis, by):
    n = lax.axis_size(axis)
    return lax.ppermute(value, axis, [(i, (i + by) % n) for i in range(n)])


def shift_open(value, axis, by):
    n = lax.axis_size(axis)
    return lax.ppermute(
        value, axis, [(i, i + by) for i in range(n) if 0 <= i + by < n]
    )


def swap(value, axis, mask):
    n = lax.axis_size(axis)
    return lax.ppermute(value, axis, [(i, i ^ mask) for i in range(n)])


def totals_scan(tot, sign):
    before = shift_open(tot, "z", sign)
    before = before + shift_open(before + tot, "z", 2 * sign)
    return before + shift_open(before + tot, "z", 4 * sign)


def across_pairs(keep, got, sign):
    total = keep + got
    return [shift_open(total, "z", sign * d) for d in (2, 4, 6)]


def back_to_pair(keep, got, others, use):
    half = ((2 * E, V), f32)
    own, partner = run(pair_kernel, [half, half], use, keep, got, *others, smem=1)
    return own, swap(partner, "z", 1)


def swap_y(blocks):
    return [blocks[0]] + [shift(blocks[s], "y", s) for s in (1, 2, 3)]


def on_device(tokens, qk_weight, conv_weight, values, cotangent):
    def place(name):
        return lax.axis_index(name).astype(jnp.int32)

    x, core, z, y = place("x"), place("core"), place("z"), place("y")
    y1, parity = y.reshape(1), lax.rem(z, 2).reshape(1)
    sel_q, sel_k = jnp.asarray(SEL_Q, bf16), jnp.asarray(SEL_K, bf16)
    w = jnp.asarray(WEIGHT, f32)
    local_x = tokens[0]
    wide = HG * V

    by_head = [((T, wide), f32)] * NY
    v_all = swap_y(run(pack_kernel, by_head, y1, values[0], smem=1))
    projected = jnp.dot(local_x, qk_weight, preferred_element_type=f32)
    halo = lax.ppermute(
        projected[T - 8 :], ("z", "y"), [(i, i + 1) for i in range(NZ * NY - 1)]
    )
    mixed = run(
        mix_kernel, [((T, 128), f32)] * NY, y1, after(projected, *v_all[1:]), halo, conv_weight, smem=1,
        scratch=[pltpu.VMEM((T + 8, 512), f32), pltpu.VMEM((NY, T, 128), f32)],
    )
    mixed = swap_y(mixed)
    uq, uk, tot = timed(
        2.6, prepare_kernel,
        [((HG, TS, 128), bf16), ((HG, TS, 128), bf16), ((8, EP), f32)],
        y1, *mixed, sel_k, w, smem=1, scratch=[pltpu.VMEM((TS, 128), f32)],
    )
    c_all = swap_y(run(pack_kernel, by_head, y1, after(cotangent[0], tot), smem=1))
    etot = totals_scan(tot, 1)
    half = ((2 * E, V), f32)
    half_scratch = [
        pltpu.VMEM((2, 2 * E, V), f32), pltpu.VMEM((NY, T, wide), f32),
        pltpu.SemaphoreType.DMA((NY,)),
    ]
    keep, send, vb, rs = timed(
        2.8, state_kernel, [half, half, ((TS, wide), bf16), ((HG, TS, V), f32)],
        parity, y1, uq, uk, *v_all, sel_k, w, smem=2, scratch=half_scratch,
        placed=(4, 5, 6, 7),
    )
    g_keep, g_send, dn, inv = timed(
        2.4, denom_kernel, [half, half, ((TS, wide), bf16), ((HG, TS, V), f32)],
        parity, y1, uq, rs, etot, *c_all, sel_q, w, smem=2, scratch=half_scratch,
        placed=(5, 6, 7, 8),
    )
    pair = swap(after(send, etot), "z", 1)
    g_pair = swap(g_send, "z", 1)
    earlier = across_pairs(keep, pair, 1)
    g_later = across_pairs(g_keep, g_pair, -1)
    own, got = back_to_pair(keep, after(pair, g_pair), earlier, parity)
    g_own, g_got = back_to_pair(g_keep, g_pair, g_later, 1 - parity)
    own = after(own, g_own)

    states = pltpu.VMEM((HG, EP, V), bf16)
    square = ((TS, 128), f32)
    out, dq, gv_in, dk, gtot = timed(
        9.5, local_kernel,
        [((NY, T, wide), f32), square, ((TS, wide), f32), square, ((8, EP), f32)],
        parity, uq, uk, vb, dn, inv, etot, own, got, sel_q, w, smem=1,
        scratch=[pltpu.VMEM((TS, 128), f32), states],
    )
    x_packed = timed(
        1.5, pack_columns_kernel, [((T, NZ * T), f32)] * NY, y1, after(local_x, etot), smem=1
    )
    x_all = swap_y(lax.optimization_barrier((*x_packed, g_keep))[:NY])
    (flipped,) = timed(1.9, flip_kernel, [((NZ * T, TS), bf16)], y1, *x_all, smem=1)
    egtot = totals_scan(gtot, -1)

    *both, gm, edge = timed(
        3.5, key_kernel, [((T, 2 * wide), f32)] * NY + [square, ((8, 128), f32)],
        parity, y1, uk, vb, gv_in, dq, dk, g_own, g_got, egtot, out, sel_k, smem=2,
        scratch=[states, pltpu.VMEM((TS, wide), f32), pltpu.SemaphoreType.DMA((2 * NY,))],
        far_outs=(0, 1, 2, 3),
    )
    taps = conv_weight.shape[0]
    cw = jnp.transpose(conv_weight.reshape(taps, 2, NY, 64), (0, 2, 1, 3)).reshape(taps, 512)
    (gp,) = run(
        conv_back_kernel, [square], y1, gm, shift_open(edge, "z", -1), cw, smem=1,
        scratch=[pltpu.VMEM((TS + 8, 128), f32)],
    )
    blocks = [gp] + [shift(gp, "y", s) for s in (1, 2, 3)]
    keep, send, grad_own = timed(
        2.0, weight_kernel,
        [((NZ * T // 2, 512), f32), ((NZ * T // 2, 512), f32), ((T, 512), bf16)],
        jnp.stack([y, core]), *blocks, flipped, smem=1,
        scratch=[pltpu.VMEM((TS, 512), bf16)],
    )
    quarter = ((T, 512), f32)
    parts = run(
        split_x_kernel, [quarter] * NX, x.reshape(1), keep, swap(send, "core", 1), smem=1
    )
    own_rows = jnp.transpose(
        after(grad_own, parts[0]).reshape(T, NY, 2, 64), (0, 2, 1, 3)
    ).reshape(T, 512)
    grad_x = mm_nt(own_rows, qk_weight).astype(bf16)
    parts = [parts[0]] + [shift(parts[s], "x", s) for s in (1, 2, 3)]
    parts[0] = after(parts[0], grad_x)
    both = swap_y(lax.optimization_barrier((*both, parts[1]))[:NY])
    mixed_out, grad_values = run(
        rows_kernel, [((T, H * V), bf16)] * 2, y1, *both, smem=1
    )
    for mask in (1, 2, 4):
        n = 64 // mask
        bit = lax.rem(lax.div(z, mask), 2).reshape(1)
        keep, send = run(
            split_z_kernel, [((n, 512), f32), ((n, 512), f32)], bit, *parts, smem=1
        )
        parts = [keep, swap(send, "z", mask)]
    (pair_rows,) = run(
        stack_kernel, [((32, 512), f32)], core.reshape(1), *parts,
        *[swap(a, "core", 1) for a in parts], smem=1,
    )
    stacks = [pair_rows] + [shift(pair_rows, "x", s) for s in (1, 2, 3)]
    stacks[0] = after(stacks[0], grad_values)
    (weight_grad,) = run(finish_kernel, [((T, 512), f32)], x.reshape(1), *stacks, smem=1)

    return (mixed_out[None], grad_x[None], grad_values[None], weight_grad)


def solution(mesh):
    inner = Mesh(mesh.devices.reshape(NX, NC, NZ, NY), ("x", "core", "z", "y"))
    rows = P(("x", "core"), ("z", "y"), None)
    return jax.shard_map(
        on_device,
        mesh=inner,
        in_specs=(rows, P(), P(), rows, rows),
        out_specs=(rows, rows, rows, P(("z", "y"), None)),
        check_vma=False,
    )
```

```python
import jax
import jax.numpy as jnp
import numpy as np
from jax import lax
from jax.experimental import pallas as pl
from jax.experimental.pallas import tpu as pltpu
from jax.sharding import Mesh, PartitionSpec as P

H = 16
F = 16
V = 128
NX, NC, NZ, NY = 4, 2, 8, 4
T = 128
TS = T * NY
HG = H // NY
E = 160
EP = 256
f32 = jnp.float32
bf16 = jnp.bfloat16


def feature_tables():
    first = np.zeros((128, 512), np.float32)
    weight = np.zeros((8, EP), np.float32)
    for f in range(128):
        i, d = f % 16, f // 16
        first[i, f] = 1
        first[(i + d) % 16, 128 + f] = 1
        weight[:, f] = 1 / 32 if d == 0 else 1 / 16
    for f in range(8):
        first[f, 256 + f] = 1
        first[f + 8, 384 + f] = 1
        weight[:, 128 + f] = 1 / 16
    for f in range(16):
        first[f, 256 + 8 + f] = 1
        first[16, 384 + 8 + f] = 0.5
        weight[:, 128 + 8 + f] = 1 / 4
    first[16, 256 + 24] = 0.5
    first[16, 384 + 24] = 0.5
    weight[:, 128 + 24] = 1
    sel_q = first.copy()
    sel_q[64:80] = first[:16]
    sel_k = first.copy()
    sel_k[32:48] = first[:16]
    return sel_q, sel_k, weight


SEL_Q, SEL_K, WEIGHT = feature_tables()
BIT_REVERSED = (0, 4, 2, 6, 1, 5, 3, 7)


def mm(a, b):
    return lax.dot_general(a, b, (((1,), (0,)), ((), ())), preferred_element_type=f32)


def mm_nt(a, b):
    return lax.dot_general(a, b, (((1,), (1,)), ((), ())), preferred_element_type=f32)


def mm_tn(a, b):
    return lax.dot_general(a, b, (((0,), (0,)), ((), ())), preferred_element_type=f32)


def run(kernel, outs, *args, scratch=(), smem=0, us=0.5, placed=(), far_outs=()):
    vm = pl.BlockSpec(memory_space=pltpu.VMEM)
    sm = pl.BlockSpec(memory_space=pltpu.SMEM)
    return pl.pallas_call(
        kernel,
        out_shape=[
            pltpu.HBM(s, d) if i in far_outs else jax.ShapeDtypeStruct(s, d)
            for i, (s, d) in enumerate(outs)
        ],
        in_specs=[
            sm if i < smem else pl.BlockSpec(memory_space=pltpu.HBM) if i in placed else vm
            for i in range(len(args))
        ],
        out_specs=[
            pl.BlockSpec(memory_space=pltpu.HBM) if i in far_outs else vm for i in range(len(outs))
        ],
        scratch_shapes=list(scratch),
        compiler_params=pltpu.CompilerParams(vmem_limit_bytes=12 << 20),
        cost_estimate=pl.CostEstimate(
            flops=0, bytes_accessed=int(us * 3.5e6), transcendentals=0
        ),
    )(
        *[
            pltpu.with_memory_space_constraint(a, pltpu.HBM) if i in placed else a
            for i, a in enumerate(args)
        ]
    )


def timed(us, *args, **kwargs):
    return run(*args, us=us, **kwargs)


def features(u, sel):
    x = mm(u, sel)
    return jnp.concatenate([x[:, :128] * x[:, 128:256], x[:, 256:384] * x[:, 384:]], 1)


def feature_grad(u, sel, grad):
    x = mm(u, sel)
    g1, g2 = grad[:, :128], grad[:, 128:]
    stacked = jnp.concatenate(
        [g1 * x[:, 128:256], g1 * x[:, :128], g2 * x[:, 384:], g2 * x[:, 256:384]], 1
    ).astype(bf16)
    return mm_nt(stacked, sel)


def causal(rows, r):
    row = lax.broadcasted_iota(jnp.int32, (T, rows), 0) + r * T
    col = lax.broadcasted_iota(jnp.int32, (T, rows), 1)
    return row >= col


def lanes(h):
    return pl.ds(pl.multiple_of(h * V, V), V)


def turned(y, s):
    return lax.rem(y[0] + (s + NY), NY)


def group_lanes(g, width):
    return pl.ds(pl.multiple_of(g * width, width), width)


def pack_kernel(y, a, *outs):
    for s, o in enumerate(outs):
        o[...] = a[:, group_lanes(turned(y, s), HG * V)].astype(f32)


def fetch(blocks, buffer, sems):
    copies = [pltpu.make_async_copy(b, buffer.at[s], sems.at[s]) for s, b in enumerate(blocks)]
    for c in copies:
        c.start()
    return copies


def after(value, *others):
    return lax.optimization_barrier((value, *others))[0]


def pack_columns_kernel(y, a, *outs):
    for s, o in enumerate(outs):
        for k in range(NZ):
            o[:, k * T : (k + 1) * T] = a[:, group_lanes(turned(y, s) + k * NY, T)].astype(f32)


def flip_kernel(y, a0, a1, a2, a3, flipped):
    for s, a in enumerate((a0, a1, a2, a3)):
        cols = group_lanes(turned(y, -s), T)
        for k in range(NZ):
            t = jnp.transpose(a[:, k * T : (k + 1) * T]).astype(bf16)
            for part in range(NC * NX):
                at = part * T + BIT_REVERSED[k] * 16
                flipped[at : at + 16, cols] = t[part * 16 : part * 16 + 16]


def mix_kernel(y, projected, halo, cw, o0, o1, o2, o3, pad, blocks):
    pad[:8] = halo[...]
    pad[8:] = projected[...]
    m = projected[...] * cw[0:1]
    for j in (1, 2):
        m += pad[8 - j : 8 - j + T] * cw[j : j + 1]
    lane = lax.broadcasted_iota(jnp.int32, (T, 128), 1)
    for g in range(NY):
        at = (g // 2) * 128
        q, k = m[:, at : at + 128], m[:, 256 + at : 256 + at + 128]
        if g % 2:
            q = pltpu.roll(q, 64, 1)
        else:
            k = pltpu.roll(k, 64, 1)
        blocks[g] = jnp.where(lane < 64, q, k)
    for s, o in enumerate((o0, o1, o2, o3)):
        o[...] = blocks[turned(y, s)]


def prepare_kernel(y, b0, b1, b2, b3, sel_k, w, uq, uk, tot, mg):
    for s, b in enumerate((b0, b1, b2, b3)):
        mg[group_lanes(turned(y, -s), T)] = b[...]
    lane = lax.broadcasted_iota(jnp.int32, (TS, 128), 1)
    tot[...] = jnp.zeros_like(tot)

    def one(h, _):
        for is_key in (0, 1):
            x = pltpu.roll(mg[...], (256 - 64 * is_key) - 16 * h, 1)
            hi = x.astype(bf16).astype(f32)
            lo = x - hi
            a, b = (lo, hi) if is_key else (hi, lo)
            u = jnp.where(lane < 16, hi, jnp.where(lane == 16, 2.0, 0.0))
            u = jnp.where((lane >= 32) & (lane < 48), pltpu.roll(a, 32, 1), u)
            u = jnp.where((lane >= 64) & (lane < 80), pltpu.roll(b, 64, 1), u)
            (uk if is_key else uq)[h] = u.astype(bf16)
        rk = features(uk[h], sel_k[...])
        tot[pl.ds(h, 1)] = jnp.sum(rk, 0, keepdims=True) * w[0:1]
        return 0

    lax.fori_loop(0, HG, one, 0)


def halves(scratch, p, keep, send):
    keep[...] = scratch[p]
    send[...] = scratch[1 - p]


def state_kernel(
    p, y, uq, uk, v0, v1, v2, v3, sel_k, w, keep, send, vb, rs, scratch, buffer, sems
):
    copies = fetch((v0, v1, v2, v3), buffer, sems)
    def sums(h, _):
        for r in range(NY):
            rows = (r + 1) * T
            t = mm_nt(uq[h, r * T : rows], uk[h, :rows])
            t = jnp.where(causal(rows, r), 0.5 + t * t * (1 / 32), 0.0)
            rs[h, r * T : rows] = jnp.broadcast_to(jnp.sum(t, 1, keepdims=True), (T, V))
        return 0

    lax.fori_loop(0, HG, sums, 0)
    for s in range(NY):
        copies[s].wait()
        vb[group_lanes(turned(y, -s), T)] = buffer[s].astype(bf16)

    def one(h, _):
        rk = (features(uk[h], sel_k[...]) * w[0:1]).astype(bf16)
        s = mm_tn(rk, vb[:, lanes(h)])
        scratch[lax.div(h, 2), pl.ds(pl.multiple_of(lax.rem(h, 2) * E, E), E)] = s[:E]
        return 0

    lax.fori_loop(0, HG, one, 0)
    halves(scratch, p[0], keep, send)


def denom_kernel(
    p, y, uq, rs, etot, c0, c1, c2, c3, sel_q, w, keep, send, dn, inv, scratch, buffer, sems
):
    for c in fetch((c0, c1, c2, c3), buffer, sems):
        c.wait()
    def one(h, _):
        rq = features(uq[h], sel_q[...])
        den = rs[h] + jnp.sum(rq * etot[pl.ds(h, 1)], 1, keepdims=True)
        iv = 1.0 / den
        inv[h] = iv
        for s in range(NY):
            rows = group_lanes(turned(y, -s), T)
            dn[rows, lanes(h)] = (buffer[s, :, lanes(h)] * inv[h, rows]).astype(bf16)
        s = mm_tn((rq * w[0:1]).astype(bf16), dn[:, lanes(h)])
        scratch[lax.div(h, 2), pl.ds(pl.multiple_of(lax.rem(h, 2) * E, E), E)] = s[:E]
        return 0

    lax.fori_loop(0, HG, one, 0)
    halves(scratch, p[0], keep, send)


def pair_kernel(use, keep, got, e0, e1, e2, own, partner):
    base = e0[...] + e1[...] + e2[...]
    own[...] = base + jnp.where(use[0] > 0, got[...], 0.0)
    partner[...] = base + jnp.where(use[0] > 0, 0.0, keep[...])


def fill_states(p, own, got, scratch):
    zero = jnp.zeros((EP - E, V), bf16)
    for which, a in ((p, own), (1 - p, got)):
        for i in range(2):
            scratch[2 * which + i, :E] = a[i * E : (i + 1) * E].astype(bf16)
            scratch[2 * which + i, E:] = zero


def local_kernel(
    p, uq, uk, vb, dn, inv, etot, own, got, sel_q, w, out, dq, gv, dk, gtot, dk_acc, states
):
    lane = lax.broadcasted_iota(jnp.int32, (TS, 128), 1)
    gtot[...] = jnp.zeros_like(gtot)
    dq[...] = jnp.zeros_like(dq)
    dk[...] = jnp.zeros_like(dk)
    fill_states(p[0], own, got, states)

    def one(h, _):
        cols = lanes(h)
        c = states[h]
        tot_row = etot[pl.ds(h, 1)]
        gsum = jnp.zeros((1, EP), f32)
        grads = []
        for r in reversed(range(NY)):
            rows = (r + 1) * T
            mine = slice(r * T, rows)
            u = uq[h, mine]
            keep = causal(rows, r)
            s = mm_nt(u, uk[h, :rows])
            pr = jnp.where(keep, 0.5 + s * s * (1 / 32), 0.0).astype(bf16)
            rq = features(u, sel_q[...])
            numer = mm(pr, vb[:rows, cols]) + mm(rq.astype(bf16), c)
            o = numer * inv[h, mine]
            out[r, :, cols] = o
            d = dn[mine, cols]
            dd = -jnp.sum(d.astype(f32) * o, 1, keepdims=True)
            dp = mm_nt(d, vb[:rows, cols]) + dd
            ds = jnp.where(keep, dp * s * (1 / 16), 0.0).astype(bf16)
            gsum += jnp.sum(rq * dd, 0, keepdims=True)
            dr = mm_nt(d, c) + dd * tot_row
            grads.append(mm(ds, uk[h, :rows]) + feature_grad(u, sel_q[...], dr))
            gv_add = mm_tn(pr, d)
            dk_add = mm_tn(ds, u)
            if r == NY - 1:
                gv[:, cols] = gv_add
                dk_acc[...] = dk_add
            else:
                gv[:rows, cols] += gv_add
                dk_acc[:rows] += dk_add
        gtot[pl.ds(h, 1)] = gsum * w[0:1]
        g = jnp.concatenate(grads[::-1], 0)
        dq[...] += pltpu.roll(jnp.where(lane < 16, g, 0.0), 16 * h, 1)
        dk[...] += pltpu.roll(jnp.where(lane < 16, dk_acc[...], 0.0), 64 + 16 * h, 1)
        return 0

    lax.fori_loop(0, HG, one, 0)


def key_kernel(
    p, y, uk, vb, gv_in, dq, dk, own, got, egtot, out, sel_k,
    o0, o1, o2, o3, gm, edge, states, gv, sems,
):
    lane = lax.broadcasted_iota(jnp.int32, (TS, 128), 1)
    copies = [
        pltpu.make_async_copy(out.at[turned(y, s)], o.at[:, pl.ds(0, HG * V)], sems.at[s])
        for s, o in enumerate((o0, o1, o2, o3))
    ]
    for c in copies:
        c.start()
    fill_states(p[0], own, got, states)
    gm[...] = dq[...] + dk[...]

    def one(h, _):
        cols = lanes(h)
        c = states[h]
        rk = features(uk[h], sel_k[...]).astype(bf16)
        gv[:, cols] = gv_in[:, cols] + mm(rk, c)
        dr = mm_nt(vb[:, cols], c) + egtot[pl.ds(h, 1)]
        g = feature_grad(uk[h], sel_k[...], dr)
        gm[...] += pltpu.roll(jnp.where(lane < 16, g, 0.0), 64 + 16 * h, 1)
        return 0

    lax.fori_loop(0, HG, one, 0)
    edge[...] = gm[:8]
    for s, o in enumerate((o0, o1, o2, o3)):
        copies.append(
            pltpu.make_async_copy(
                gv.at[group_lanes(turned(y, s), T)], o.at[:, pl.ds(HG * V, HG * V)], sems.at[NY + s]
            )
        )
        copies[-1].start()
    for c in copies:
        c.wait()


def conv_back_kernel(y, gm, halo, cw, gp, pad):
    pad[:TS] = gm[...]
    pad[TS:] = halo[...]
    cols = group_lanes(y[0], 128)
    total = gm[...] * cw[0:1, cols]
    for j in (1, 2):
        total += pad[j : TS + j] * cw[j : j + 1, cols]
    gp[...] = total


def weight_kernel(at, g0, g1, g2, g3, flipped, keep, send, grad_own, gp):
    y, core = at[0], at[1]
    for s, g in enumerate((g0, g1, g2, g3)):
        gp[:, group_lanes(turned(at, -s), 128)] = g[...].astype(bf16)
    half = NZ * T // 2
    for which, ref in ((1 - core, send), (core, keep)):
        ref[...] = mm(flipped[group_lanes(which, half)], gp[...])
    grad_own[...] = gp[group_lanes(y, T)]


def split_x_kernel(x, a, b, o0, o1, o2, o3):
    for s, o in enumerate((o0, o1, o2, o3)):
        rows = pl.ds(pl.multiple_of(lax.rem(x[0] + s, NX) * T, T), T)
        o[...] = a[rows] + b[rows]


def split_z_kernel(bit, *refs):
    ins, (keep, send) = refs[:-2], refs[-2:]
    n = keep.shape[0]
    for which, o in ((bit[0], keep), (1 - bit[0], send)):
        rows = pl.ds(pl.multiple_of(which * n, n), n)
        total = ins[0][rows]
        for a in ins[1:]:
            total += a[rows]
        o[...] = total


def stack_kernel(core, a, b, c, d, o):
    total = a[...] + b[...]
    o[group_lanes(core[0], 16)] = total
    o[group_lanes(1 - core[0], 16)] = c[...] + d[...]


def finish_kernel(x, m0, m1, m2, m3, rows):
    lane = lax.broadcasted_iota(jnp.int32, (16, 128), 1)
    for s, m in enumerate((m0, m1, m2, m3)):
        src = lax.rem(x[0] - s + NX, NX)
        for core in range(NC):
            at = pl.ds(pl.multiple_of(core * 64 + src * 16, 16), 16)
            b = m[core * 16 : core * 16 + 16]
            for half in range(2):
                lo, hi = b[:, half * 256 : half * 256 + 128], b[:, half * 256 + 128 : half * 256 + 256]
                q = jnp.where(lane < 64, lo, pltpu.roll(hi, 64, 1))
                k = jnp.where(lane < 64, pltpu.roll(lo, 64, 1), hi)
                rows[at, half * 128 : half * 128 + 128] = q
                rows[at, 256 + half * 128 : 256 + half * 128 + 128] = k


def rows_kernel(y, b0, b1, b2, b3, out, grad):
    for s, b in enumerate((b0, b1, b2, b3)):
        cols = group_lanes(turned(y, -s), HG * V)
        out[:, cols] = b[:, : HG * V].astype(bf16)
        grad[:, cols] = b[:, HG * V :].astype(bf16)


def shift(value, axis, by):
    n = lax.axis_size(axis)
    return lax.ppermute(value, axis, [(i, (i + by) % n) for i in range(n)])


def shift_open(value, axis, by):
    n = lax.axis_size(axis)
    return lax.ppermute(
        value, axis, [(i, i + by) for i in range(n) if 0 <= i + by < n]
    )


def swap(value, axis, mask):
    n = lax.axis_size(axis)
    return lax.ppermute(value, axis, [(i, i ^ mask) for i in range(n)])


def totals_scan(tot, sign, steps):
    before = jnp.zeros_like(tot)
    for d in steps:
        before = before + shift_open(before + tot, "z", d * sign)
    return before


def across_pairs(keep, got, sign):
    total = keep + got
    return [shift_open(total, "z", sign * d) for d in (2, 4, 6)]


def back_to_pair(keep, got, others, use):
    half = ((2 * E, V), f32)
    own, partner = run(pair_kernel, [half, half], use, keep, got, *others, smem=1)
    return own, swap(partner, "z", 1)


def swap_y(blocks):
    return [blocks[0]] + [shift(blocks[s], "y", s) for s in (1, 2, 3)]


def on_device(tokens, qk_weight, conv_weight, values, cotangent):
    def place(name):
        return lax.axis_index(name).astype(jnp.int32)

    x, core, z, y = place("x"), place("core"), place("z"), place("y")
    y1, parity = y.reshape(1), lax.rem(z, 2).reshape(1)
    sel_q, sel_k = jnp.asarray(SEL_Q, bf16), jnp.asarray(SEL_K, bf16)
    w = jnp.asarray(WEIGHT, f32)
    local_x = tokens[0]
    wide = HG * V

    by_head = [((T, wide), f32)] * NY
    v_all = swap_y(run(pack_kernel, by_head, y1, values[0], smem=1))
    projected = jnp.dot(local_x, qk_weight, preferred_element_type=f32)
    halo = lax.ppermute(
        projected[T - 8 :], ("z", "y"), [(i, i + 1) for i in range(NZ * NY - 1)]
    )
    mixed = run(
        mix_kernel, [((T, 128), f32)] * NY, y1, after(projected, *v_all[1:]), halo, conv_weight, smem=1,
        scratch=[pltpu.VMEM((T + 8, 512), f32), pltpu.VMEM((NY, T, 128), f32)],
    )
    mixed = swap_y(mixed)
    uq, uk, tot = timed(
        2.6, prepare_kernel,
        [((HG, TS, 128), bf16), ((HG, TS, 128), bf16), ((8, EP), f32)],
        y1, *mixed, sel_k, w, smem=1, scratch=[pltpu.VMEM((TS, 128), f32)],
    )
    c_all = swap_y(run(pack_kernel, by_head, y1, after(cotangent[0], tot), smem=1))
    etot = totals_scan(tot, 1, (1, 2, 4))
    half = ((2 * E, V), f32)
    half_scratch = [
        pltpu.VMEM((2, 2 * E, V), f32), pltpu.VMEM((NY, T, wide), f32),
        pltpu.SemaphoreType.DMA((NY,)),
    ]
    keep, send, vb, rs = timed(
        2.8, state_kernel, [half, half, ((TS, wide), bf16), ((HG, TS, V), f32)],
        parity, y1, uq, uk, *v_all, sel_k, w, smem=2, scratch=half_scratch,
        placed=(4, 5, 6, 7),
    )
    g_keep, g_send, dn, inv = timed(
        2.4, denom_kernel, [half, half, ((TS, wide), bf16), ((HG, TS, V), f32)],
        parity, y1, uq, rs, etot, *c_all, sel_q, w, smem=2, scratch=half_scratch,
        placed=(5, 6, 7, 8),
    )
    pair = swap(after(send, etot), "z", 1)
    g_pair = swap(g_send, "z", 1)
    earlier = across_pairs(keep, pair, 1)
    g_later = across_pairs(g_keep, g_pair, -1)
    own, got = back_to_pair(keep, after(pair, g_pair), earlier, parity)
    g_own, g_got = back_to_pair(g_keep, g_pair, g_later, 1 - parity)
    own = after(own, g_own)

    states = pltpu.VMEM((HG, EP, V), bf16)
    square = ((TS, 128), f32)
    out, dq, gv_in, dk, gtot = timed(
        9.5, local_kernel,
        [((NY, T, wide), f32), square, ((TS, wide), f32), square, ((8, EP), f32)],
        parity, uq, uk, vb, dn, inv, etot, own, got, sel_q, w, smem=1,
        scratch=[pltpu.VMEM((TS, 128), f32), states],
    )
    x_packed = timed(
        1.5, pack_columns_kernel, [((T, NZ * T), f32)] * NY, y1, after(local_x, etot), smem=1
    )
    x_all = swap_y(lax.optimization_barrier((*x_packed, g_keep))[:NY])
    (flipped,) = timed(1.9, flip_kernel, [((NZ * T, TS), bf16)], y1, *x_all, smem=1)
    egtot = totals_scan(gtot, -1, (4, 2, 1))

    *both, gm, edge = timed(
        3.5, key_kernel, [((T, 2 * wide), f32)] * NY + [square, ((8, 128), f32)],
        parity, y1, uk, vb, gv_in, dq, dk, g_own, g_got, egtot, out, sel_k, smem=2,
        scratch=[states, pltpu.VMEM((TS, wide), f32), pltpu.SemaphoreType.DMA((2 * NY,))],
        far_outs=(0, 1, 2, 3),
    )
    taps = conv_weight.shape[0]
    cw = jnp.transpose(conv_weight.reshape(taps, 2, NY, 64), (0, 2, 1, 3)).reshape(taps, 512)
    (gp,) = run(
        conv_back_kernel, [square], y1, gm, shift_open(edge, "z", -1), cw, smem=1,
        scratch=[pltpu.VMEM((TS + 8, 128), f32)],
    )
    blocks = [gp] + [shift(gp, "y", s) for s in (1, 2, 3)]
    keep, send, grad_own = timed(
        2.0, weight_kernel,
        [((NZ * T // 2, 512), f32), ((NZ * T // 2, 512), f32), ((T, 512), bf16)],
        jnp.stack([y, core]), *blocks, flipped, smem=1,
        scratch=[pltpu.VMEM((TS, 512), bf16)],
    )
    quarter = ((T, 512), f32)
    parts = run(
        split_x_kernel, [quarter] * NX, x.reshape(1), keep, swap(send, "core", 1), smem=1
    )
    parts = [parts[0]] + [shift(parts[s], "x", s) for s in (1, 2, 3)]
    both = swap_y(lax.optimization_barrier((*both, parts[1]))[:NY])
    mixed_out, grad_values = run(
        rows_kernel, [((T, H * V), bf16)] * 2, y1, *both, smem=1
    )
    for mask in (1, 2, 4):
        n = 64 // mask
        bit = lax.rem(lax.div(z, mask), 2).reshape(1)
        keep, send = run(
            split_z_kernel, [((n, 512), f32), ((n, 512), f32)], bit, *parts, smem=1
        )
        if mask == 1:
            own_rows = jnp.transpose(
                after(grad_own, keep).reshape(T, NY, 2, 64), (0, 2, 1, 3)
            ).reshape(T, 512)
            grad_x = mm_nt(own_rows, qk_weight).astype(bf16)
            parts = [after(keep, grad_x), swap(send, "z", mask)]
        else:
            parts = [keep, swap(send, "z", mask)]
    (pair_rows,) = run(
        stack_kernel, [((32, 512), f32)], core.reshape(1), *parts,
        *[swap(a, "core", 1) for a in parts], smem=1,
    )
    stacks = [pair_rows] + [shift(pair_rows, "x", s) for s in (1, 2, 3)]
    stacks[0] = after(stacks[0], grad_values)
    (weight_grad,) = run(finish_kernel, [((T, 512), f32)], x.reshape(1), *stacks, smem=1)

    return (mixed_out[None], grad_x[None], grad_values[None], weight_grad)


def solution(mesh):
    inner = Mesh(mesh.devices.reshape(NX, NC, NZ, NY), ("x", "core", "z", "y"))
    rows = P(("x", "core"), ("z", "y"), None)
    return jax.shard_map(
        on_device,
        mesh=inner,
        in_specs=(rows, P(), P(), rows, rows),
        out_specs=(rows, rows, rows, P(("z", "y"), None)),
        check_vma=False,
    )
```
